512 devices in a mesh: bx: 16 (over z), by: 32 (over x, y, core).
Axes of the slice: x: 4, y: 4, z: 16, core: 2. Of those that a mesh axis runs over, the one named last changes fastest.
Arguments:
- rhs: float32 [32, 64, 256, 384], P('bx', 'by'), may hold values from -6 to 6
- perm1: int32 [32, 64, 256], P('bx', 'by'), may hold values from 0 to 255, each once within a row
- interp1: bfloat16 [32, 64, 160, 96], P('bx', 'by'), may hold values from -0.5 to 0.5
- pivinv1: bfloat16 [32, 64, 160, 160], P('bx', 'by'), may hold values from -0.5 to 0.5
- couple1: bfloat16 [32, 64, 8, 96, 160], P('bx', 'by'), may hold values from -0.15625 to 0.15625
- perm2: int32 [16, 32, 384], P('bx', 'by'), may hold values from 0 to 383, each once within a row
- interp2: bfloat16 [16, 32, 256, 128], P('bx', 'by'), may hold values from -0.375 to 0.375
- pivinv2: bfloat16 [16, 32, 256, 256], P('bx', 'by'), may hold values from -0.375 to 0.375
- couple2: bfloat16 [16, 32, 8, 128, 256], P('bx', 'by'), may hold values from -0.125 to 0.125
Outputs:
- red1: bfloat16 [32, 64, 160, 384], P('bx', 'by')
- red2: bfloat16 [16, 32, 256, 384], P('bx', 'by')
- skel2: float32 [16, 32, 128, 384], P('bx', 'by')
The draws below stay inside these ranges and needn't reach their ends.
Inputs may be any that keep to these rules, and one draw needn't show every extreme that they name: Each row of perm1 holds every point index once. Each row of perm2 holds every point index once.
All inputs are finite; a program needn't handle non-finite values.
Results may differ from the reference program's by a relative error of at most 0.013.
Values may be sent and summed in bfloat16 or wider, within the bound.
No kernel may reach another device: no remote copies, remote signals or barrier semaphores. Data moves between devices by JAX's collectives and lax.ppermute only.
A program may use at most 64 MiB of HBM per device.

```python
import jax
import jax.numpy as jnp
from jax import lax

S1 = 96
R1 = 160
S2 = 128
K = 384
P1 = 256
P2 = 384
R2 = 256
NBX = 32
NBY = 64
NPX = 16
NPY = 32


def levels(stream_key, dims, cuts, low, top_value):
    gain, own = 1.0, jax.random.fold_in(stream_key, 6)
    for axis_at, parts in cuts:
        heights = jnp.exp(jax.random.uniform(jax.random.fold_in(own, axis_at), (parts,), jnp.float32, low / len(cuts), top_value / len(cuts)))
        gain = gain * jnp.repeat(heights, dims[axis_at] // parts).reshape([-1 if axis == axis_at else 1 for axis in range(len(dims))])
    return gain


def noise(rng, dims, spread, limit, cuts=(), kind=jnp.bfloat16):
    gain = levels(rng, dims, cuts, -0.22, 0.18) if cuts else 1.0
    array = jax.random.normal(rng, dims, jnp.float32) * spread * gain
    return jnp.minimum(jnp.maximum(array, -limit), limit).astype(kind)


def setup_inputs(seed: int = 0) -> dict:
    key_list = jax.random.split(jax.random.key(seed), 10)
    return {
        "rhs": noise(key_list[0], (NBX, NBY, P1, K), 1.0, 6.0, ((0, 16), (1, 32)), jnp.float32),
        "perm1": jax.vmap(lambda own: jax.random.permutation(own, P1))(jax.random.split(key_list[1], NBX * NBY)).reshape((NBX, NBY, P1)).astype(jnp.int32),
        "interp1": noise(key_list[2], (NBX, NBY, R1, S1), R1 ** -0.5, 0.5, ((0, 16), (1, 32))),
        "pivinv1": noise(key_list[3], (NBX, NBY, R1, R1), R1 ** -0.5, 0.5, ((0, 16), (1, 32))),
        "couple1": noise(key_list[4], (NBX, NBY, 8, S1, R1), (8 * R1) ** -0.5, 0.15625, ((0, 16), (1, 32))),
        "perm2": jax.vmap(lambda own: jax.random.permutation(own, P2))(jax.random.split(key_list[5], NPX * NPY)).reshape((NPX, NPY, P2)).astype(jnp.int32),
        "interp2": noise(key_list[6], (NPX, NPY, R2, S2), R2 ** -0.5, 0.375, ((0, 16), (1, 32))),
        "pivinv2": noise(key_list[7], (NPX, NPY, R2, R2), R2 ** -0.5, 0.375, ((0, 16), (1, 32))),
        "couple2": noise(key_list[8], (NPX, NPY, 8, S2, R2), (8 * R2) ** -0.5, 0.125, ((0, 16), (1, 32))),
    }


OFFSETS = [(-1, -1), (-1, 0), (-1, 1), (0, -1), (0, 1), (1, -1), (1, 0), (1, 1)]


def rounded(value):
    return lax.optimization_barrier(value.astype(jnp.bfloat16)).astype(jnp.float32)


def eliminate(skel, red, interp, pivinv, couple):
    rows, cols = skel.shape[0], skel.shape[1]
    zall = jnp.zeros(red.shape, jnp.bfloat16)
    for color in range(4):
        a, b = color // 2, color % 2
        skel_c = skel[a::2, b::2]
        tmat = interp[a::2, b::2].astype(jnp.float32)
        diff = red[a::2, b::2] - jnp.einsum('ijrs,ijsk->ijrk', tmat, rounded(skel_c))
        zc = jnp.einsum('ijrq,ijqk->ijrk', pivinv[a::2, b::2].astype(jnp.float32), rounded(diff)).astype(jnp.bfloat16)
        zf = zc.astype(jnp.float32)
        skel = skel.at[a::2, b::2].set(skel_c - jnp.einsum('ijrs,ijrk->ijsk', tmat, zf))
        zall = zall.at[a::2, b::2].set(zc)
        zgrid = jnp.zeros(red.shape, jnp.bfloat16).at[a::2, b::2].set(zc)
        zpad = jnp.pad(zgrid, ((1, 1), (1, 1), (0, 0), (0, 0)))
        for k in range(8):
            dx, dy = OFFSETS[k]
            pa, pb = (a - dx) % 2, (b - dy) % 2
            source = zpad[1 + dx:1 + dx + rows, 1 + dy:1 + dy + cols][pa::2, pb::2].astype(jnp.float32)
            update = jnp.einsum('ijsr,ijrk->ijsk', couple[pa::2, pb::2, k].astype(jnp.float32), source)
            skel = skel.at[pa::2, pb::2].add(-update)
    return skel, zall


def reference(rhs, perm1, interp1, pivinv1, couple1, perm2, interp2, pivinv2, couple2):
    leaf = jnp.take_along_axis(rhs, perm1[:, :, :, None], axis=2)
    skel_leaf, red1 = eliminate(leaf[:, :, :S1], leaf[:, :, S1:], interp1, pivinv1, couple1)
    parents = skel_leaf.reshape(NPX, 2, NPY, 2, S1, K).transpose(0, 2, 1, 3, 4, 5).reshape(NPX, NPY, P2, K)
    parent = jnp.take_along_axis(parents, perm2[:, :, :, None], axis=2)
    skel2, red2 = eliminate(parent[:, :, :S2], parent[:, :, S2:], interp2, pivinv2, couple2)
    return red1, red2, skel2
```

```python
import functools

import jax
import jax.numpy as jnp
from jax import lax
from jax.experimental import pallas as pl
from jax.experimental.pallas import tpu as pltpu
from jax.sharding import PartitionSpec as P

S1, R1, P1 = 96, 160, 256
S2, R2, P2 = 128, 256, 384
K = 384
OFFSETS = [(-1, -1), (-1, 0), (-1, 1), (0, -1), (0, 1), (1, -1), (1, 0), (1, 1)]
BOXES = [(0, 0), (0, 1), (1, 0), (1, 1)]
F32, BF16 = jnp.float32, jnp.bfloat16


def dot(a, b):
    return lax.dot_general(a, b, (((1,), (0,)), ((), ())), preferred_element_type=F32)


def dot_t(a, b):
    return lax.dot_general(a, b, (((0,), (0,)), ((), ())), preferred_element_type=F32)


def source(box, k):
    row, col = box[0] + OFFSETS[k][0], box[1] + OFFSETS[k][1]
    return (row % 2) * 2 + col % 2, (row // 2, col // 2)


def reordered(x, perm, rows):
    pick = (lax.broadcasted_iota(jnp.int32, (rows, rows), 0) == perm).astype(F32).astype(BF16)
    high = x.astype(BF16)
    low = (x - high.astype(F32)).astype(BF16)
    return dot_t(pick, high) + dot_t(pick, low)


def call(body, ins, outs, name, scalars=0):
    specs = [pl.BlockSpec(memory_space=pltpu.SMEM)] * scalars + [pl.BlockSpec(memory_space=pltpu.VMEM)] * (
        len(ins) - scalars
    )
    return pl.pallas_call(
        body,
        out_shape=[jax.ShapeDtypeStruct(s, d) for s, d in outs],
        in_specs=specs,
        out_specs=[pl.BlockSpec(memory_space=pltpu.VMEM)] * len(outs),
        compiler_params=pltpu.CompilerParams(vmem_limit_bytes=20 * 1024 * 1024),
        cost_estimate=pl.CostEstimate(flops=300_000_000, bytes_accessed=2_000_000, transcendentals=0),
        name=name,
    )(*ins)


def pairs(dx, dy, colour=None):
    nx, ny = lax.axis_size("bx"), lax.axis_size("by")
    out = []
    for i in range(nx):
        for j in range(ny):
            if colour is not None and (i % 2) * 2 + j % 2 != colour:
                continue
            if 0 <= i + dx < nx and 0 <= j + dy < ny:
                out.append((i * ny + j, (i + dx) * ny + j + dy))
    return out


def send(z, offset, colour=None):
    return lax.ppermute(z, ("bx", "by"), pairs(-offset[0], -offset[1], colour))


def first_body(rhs, perm, interp, piv, z_out, skel_out):
    leaf = reordered(rhs[0, 0], perm[0, 0:1, :], P1)
    skel = leaf[:S1]
    diff = leaf[S1:] - dot(interp[0, 0], skel.astype(BF16))
    z_out[...] = dot(piv[0, 0], diff.astype(BF16)).astype(BF16)
    skel_out[...] = skel


def spread_body(rhs, perm, interp, couple, z, skel0, s0, s1, s2, s3, r1, r2, r3):
    zc = z[...]
    s0[...] = skel0[...] - dot_t(interp[0, 0], zc)
    for n, (s, r) in ((1, (s1, r1)), (2, (s2, r2)), (3, (s3, r3))):
        i, j = BOXES[n]
        leaf = reordered(rhs[i, j], perm[i, j : j + 1, :], P1)
        r[...] = leaf[S1:]
        acc = leaf[:S1]
        for k in range(8):
            if source((i, j), k) == (0, (0, 0)):
                acc = acc - dot_t(couple[i, j, k], zc)
        s[...] = acc


def solve_body(box, ks, interp, piv, couple, skel, red, *rest):
    zs, (z_out, skel_out) = rest[: len(ks)], rest[len(ks) :]
    i, j = box
    acc = skel[...]
    total = None
    for k, z in zip(ks, zs):
        term = dot_t(couple[i, j, k], z[...])
        total = term if total is None else total + term
    acc = acc - total
    diff = red[...] - dot(interp[i, j], acc.astype(BF16))
    z_out[...] = dot(piv[i, j], diff.astype(BF16)).astype(BF16)
    skel_out[...] = acc


def update_body(own, jobs, n_z, interp, couple, *refs):
    zs, skels, outs = refs[:n_z], refs[n_z : n_z + 4], refs[n_z + 4 :]
    for n in range(4):
        i, j = BOXES[n]
        acc = skels[n][...]
        if n == own:
            acc = acc - dot_t(interp[i, j], zs[0][...])
        for k, at in jobs[n]:
            acc = acc - dot_t(couple[i, j, k], zs[at][...])
        outs[n][...] = acc


def shards(rhs, perm1, interp1, pivinv1, couple1, perm2, interp2, pivinv2, couple2):
    leaf_s, leaf_r, leaf_z = ((S1, K), F32), ((R1, K), F32), ((R1, K), BF16)
    couple1 = couple1.swapaxes(3, 4)
    have = {}

    def jobs_of(keys, boxes=(0, 1, 2, 3)):
        order = list(keys)
        jobs = [[], [], [], []]
        for n in boxes:
            for k in range(8):
                where = source(BOXES[n], k)
                if where in order:
                    jobs[n].append((k, order.index(where)))
        return jobs

    def solve(colour, keys, skels, reds):
        box = BOXES[colour]
        ks, zs = [], []
        for k in range(8):
            if source(box, k) in keys:
                ks.append(k)
                zs.append(have[source(box, k)])
        z, skel = call(
            functools.partial(solve_body, box, ks),
            [interp1, pivinv1, couple1, skels[colour], reds[colour], *zs],
            [leaf_z, leaf_s],
            f"leaf{colour}",
        )
        have[(colour, (0, 0))] = z
        skels = list(skels)
        skels[colour] = skel
        return z, skels

    def update(own, keys, skels, drop=()):
        order = [(own, (0, 0)), *keys]
        jobs = jobs_of(order)
        for n, key in drop:
            jobs[n] = [(k, at) for k, at in jobs[n] if order[at] != key]
        return call(
            functools.partial(update_body, own, jobs, len(order)),
            [interp1, couple1, *[have[key] for key in order], *skels],
            [leaf_s] * 4,
            f"spread{own}",
        )

    z00, skel0 = call(first_body, [rhs, perm1, interp1, pivinv1], [leaf_z, leaf_s], "leaf0")
    have[(0, (0, 0))] = z00
    have[(0, (0, 1))] = send(z00, (0, 1))
    have[(0, (1, 0))] = send(z00, (1, 0))
    s0, s1, s2, s3, r1, r2, r3 = call(
        spread_body, [rhs, perm1, interp1, couple1, z00, skel0], [leaf_s] * 4 + [leaf_r] * 3, "spread0"
    )
    reds = [None, r1, r2, r3]
    z01, skels = solve(1, {(0, (0, 1))}, [s0, s1, s2, s3], reds)
    for offset in ((0, -1), (1, 0), (1, -1)):
        have[(1, offset)] = send(z01, offset)
    skels = update(1, [(0, (0, 1))], skels, drop=[(1, (0, (0, 1)))])
    z10, skels = solve(2, {(1, (0, -1)), (1, (1, 0)), (1, (1, -1)), (0, (1, 0))}, skels, reds)
    have[(2, (0, 1))] = send(z10, (0, 1))
    have[(0, (1, 1))] = send(z00, (1, 1))
    have[(2, (-1, 0))] = send(z10, (-1, 0))
    have[(2, (-1, 1))] = send(z10, (-1, 1))
    skels = update(
        2,
        [(1, (0, -1)), (1, (1, 0)), (0, (1, 0))],
        skels,
        drop=[(2, (1, (0, -1))), (2, (1, (1, 0))), (2, (0, (1, 0)))],
    )
    z11, skels = solve(3, {(2, (0, 1)), (0, (1, 1))}, skels, reds)
    for offset in ((0, -1), (-1, 0), (-1, -1)):
        have[(3, offset)] = send(z11, offset)
    skels = update(3, [(2, (0, 1)), (2, (-1, 0)), (2, (-1, 1))], skels, drop=[(3, (2, (0, 1)))])
    red1 = jnp.stack([z00, z01, z10, z11]).reshape(2, 2, R1, K)

    colour = ((lax.axis_index("bx") % 2) * 2 + lax.axis_index("by") % 2).astype(jnp.int32).reshape(1)
    par_s, par_r, par_z = ((S2, K), F32), ((R2, K), F32), ((R2, K), BF16)
    last = [(3, (0, -1)), (3, (-1, 0)), (3, (-1, -1))]
    last_jobs = jobs_of(last)

    def solve_parent(interp, piv, skel, red):
        diff = red - dot(interp[0, 0], skel.astype(BF16))
        return dot(piv[0, 0], diff.astype(BF16)).astype(BF16)

    def join_body(me, perm, interp, piv, couple, za, zb, zc, ca, cb, cc, cd, skel_out, red_out, z_out):
        zs = [za, zb, zc]
        parts = []
        for n, c in enumerate((ca, cb, cc, cd)):
            acc = c[...]
            for k, at in last_jobs[n]:
                acc = acc - dot_t(couple[BOXES[n][0], BOXES[n][1], k], zs[at][...])
            parts.append(acc)
        parent = reordered(jnp.concatenate(parts, axis=0), perm[0], P2)
        skel_out[...] = parent[:S2]
        red_out[...] = parent[S2:]

        @pl.when(me[0] == 0)
        def _():
            z_out[...] = solve_parent(interp, piv, parent[:S2], parent[S2:])

    skel, red, z = call(
        join_body,
        [colour, perm2, interp2, pivinv2, couple1, *[have[key] for key in last], *skels],
        [par_s, par_r, par_z],
        "join",
        scalars=1,
    )
    sides, ends = [3, 4], [1, 6]
    corners = [0, 2, 5, 7]
    got, zs = {}, [z]

    def scatter(c, ks):
        for k in ks:
            got[(c, k)] = send(zs[c], OFFSETS[k], c)

    def parent_body(c, keys, me, interp, piv, couple, skel, red, *rest):
        xs, (z_out, skel_out) = rest[: len(keys)], rest[len(keys) :]
        skel_out[...] = skel[...]

        @pl.when(me[0] == c)
        def _():
            total = None
            for (_, k), x in zip(keys, xs):
                term = dot(couple[0, 0, k], x[...])
                total = term if total is None else total + term
            acc = skel[...] - total
            z_out[...] = solve_parent(interp, piv, acc, red[...])
            skel_out[...] = acc

    def parent(c, keys, skel):
        z, skel = call(
            functools.partial(parent_body, c, keys),
            [colour, interp2, pivinv2, couple2, skel, red, *[got[key] for key in keys]],
            [par_z, par_s],
            f"parent{c}",
            scalars=1,
        )
        zs.append(z)
        return skel

    scatter(0, sides + ends + corners)
    skel = parent(1, [(0, k) for k in sides], skel)
    scatter(1, corners + ends + sides)
    skel = parent(2, [(0, k) for k in ends] + [(1, k) for k in corners], skel)
    scatter(2, sides + ends + corners)
    skel = parent(3, [(0, k) for k in corners] + [(1, k) for k in ends] + [(2, k) for k in sides], skel)
    scatter(3, corners + ends + sides)

    early = {0: [(1, k) for k in sides] + [(2, k) for k in ends], 1: [(2, k) for k in corners], 2: [], 3: []}
    late = {0: [(3, k) for k in corners], 1: [(3, k) for k in ends], 2: [(3, k) for k in sides], 3: []}

    def early_body(me, interp, couple, skel, z0, z1, z2, z3, *rest):
        keys = early[0] + early[1]
        xs, (skel_out, z_out) = dict(zip(keys, rest)), rest[len(keys) :]
        for c, own in enumerate((z0, z1, z2, z3)):

            @pl.when(me[0] == c)
            def _():
                zc = own[...]
                z_out[...] = zc
                acc = skel[...] - dot_t(interp[0, 0], zc)
                for key in early[c]:
                    acc = acc - dot(couple[0, 0, key[1]], xs[key][...])
                skel_out[...] = acc

    skel, red2 = call(
        early_body,
        [colour, interp2, couple2, skel, *zs, *[got[key] for key in early[0] + early[1]]],
        [par_s, par_z],
        "early",
        scalars=1,
    )

    def late_body(me, couple, skel, *rest):
        keys = late[0] + late[1] + late[2]
        xs, skel_out = dict(zip(keys, rest)), rest[len(keys)]
        for c in range(4):

            @pl.when(me[0] == c)
            def _():
                acc = skel[...]
                for key in late[c]:
                    acc = acc - dot(couple[0, 0, key[1]], xs[key][...])
                skel_out[...] = acc

    (skel2,) = call(
        late_body,
        [colour, couple2, skel, *[got[key] for key in late[0] + late[1] + late[2]]],
        [par_s],
        "late",
        scalars=1,
    )
    return (red1, red2[None, None], skel2[None, None])


def solution(mesh):
    in_specs = (
        P("bx", "by", None, None),
        P("bx", "by", None),
        P("bx", "by", None, None),
        P("bx", "by", None, None),
        P("bx", "by", None, None, None),
        P("bx", "by", None),
        P("bx", "by", None, None),
        P("bx", "by", None, None),
        P("bx", "by", None, None, None),
    )
    out_specs = (P("bx", "by", None, None), P("bx", "by", None, None), P("bx", "by", None, None))
    return jax.shard_map(shards, mesh=mesh, in_specs=in_specs, out_specs=out_specs, check_vma=False)
```

```python
import functools

import jax
import jax.numpy as jnp
from jax import lax
from jax.experimental import pallas as pl
from jax.experimental.pallas import tpu as pltpu
from jax.sharding import PartitionSpec as P


S1, R1, P1 = 96, 160, 256
S2, R2, P2 = 128, 256, 384
K = 384
OFFSETS = [(-1, -1), (-1, 0), (-1, 1), (0, -1), (0, 1), (1, -1), (1, 0), (1, 1)]
BOXES = [(0, 0), (0, 1), (1, 0), (1, 1)]
F32, BF16 = jnp.float32, jnp.bfloat16
LEAF_S, LEAF_R, LEAF_Z = ((S1, K), F32), ((R1, K), F32), ((R1, K), BF16)
LEAF_W, LEAF_M = ((5, R1, S1), BF16), ((2 * S1, K), BF16)
PAR_S, PAR_R, PAR_Z, PAR_M = ((S2, K), F32), ((R2, K), F32), ((R2, K), BF16), ((S2, K), BF16)


UP_TERMS = [((1, 0), (6, 7), (0, 1)), ((1, 1), (5, 6, 7), (0, 1, 2))]
DOWN_TERMS = [((0, 0), (1, 2), (0, 1)), ((0, 1), (0, 1, 2), (0, 1, 2))]

PACKS = {
    (1, 1): (6, 2, (0, 1)),
    (1, -1): (5, 1, (1,)),
    (1, 0): (5, 3, (0, 1, 2)),
    (-1, 1): (1, 2, (0, 1)),
    (-1, -1): (0, 1, (1,)),
    (-1, 0): (0, 3, (0, 1, 2)),
}
CORNERS = [(-1, -1), (-1, 1), (1, -1), (1, 1)]
ENDS = [(-1, 0), (1, 0)]


def dot(a, b):
    return lax.dot_general(a, b, (((1,), (0,)), ((), ())), preferred_element_type=F32)


def dot_t(a, b):
    return lax.dot_general(a, b, (((0,), (0,)), ((), ())), preferred_element_type=F32)


def source(box, k):
    row, col = box[0] + OFFSETS[k][0], box[1] + OFFSETS[k][1]
    return (row % 2) * 2 + col % 2, (row // 2, col // 2)


def reordered(x, perm, rows):
    pick = (lax.broadcasted_iota(jnp.int32, (rows, rows), 0) == perm).astype(F32).astype(BF16)
    high = x.astype(BF16)
    low = (x - high.astype(F32)).astype(BF16)
    return dot_t(pick, high) + dot_t(pick, low)


SMEM, VMEM, ANY, HBM = (pl.BlockSpec(memory_space=s) for s in (pltpu.SMEM, pltpu.VMEM, pl.ANY, pltpu.HBM))


def call(body, ins, outs, specs=(), scratch=()):
    specs = list(specs) + [VMEM] * (len(ins) - len(specs))
    return pl.pallas_call(
        body,
        out_shape=[jax.ShapeDtypeStruct(s, d) for s, d in outs],
        in_specs=specs,
        out_specs=[VMEM] * len(outs),
        scratch_shapes=list(scratch),
        compiler_params=pltpu.CompilerParams(vmem_limit_bytes=20 * 1024 * 1024),
        cost_estimate=pl.CostEstimate(flops=300_000_000, bytes_accessed=2_000_000, transcendentals=0),
    )(*ins)


def pairs(dx, dy, colours):
    nx, ny = lax.axis_size("bx"), lax.axis_size("by")
    out = []
    for i in range(nx):
        for j in range(ny):
            if (i % 2) * 2 + j % 2 in colours and 0 <= i + dx < nx and 0 <= j + dy < ny:
                out.append((i * ny + j, (i + dx) * ny + j + dy))
    return out


def shift(x, to, colours=(0, 1, 2, 3)):
    return lax.ppermute(x, ("bx", "by"), pairs(*to, colours))


def after(x, value):
    return lax.optimization_barrier((x, value))


def first_body(rhs, perm, interp, piv, couple, top, z_out, skel_out, up_out, down_out, *rest):
    packs, (x, p, t, v, sems) = rest[:6], rest[6:]
    jobs = [(rhs.at[0, 0], x), (perm, p), (interp.at[0, 0], t), (piv.at[0, 0], v)]
    for terms, out in ((UP_TERMS, up_out), (DOWN_TERMS, down_out)):
        at = 0
        for (i, j), ks, _ in terms:
            jobs.append((couple.at[i, j, pl.ds(ks[0], len(ks))], out.at[pl.ds(at, len(ks))]))
            at += len(ks)
    for (k, n, _), out in zip(PACKS.values(), packs):
        jobs.append((top.at[0, 0, pl.ds(k, n)], out))
    copies = [pltpu.make_async_copy(a, b, sems.at[n]) for n, (a, b) in enumerate(jobs)]
    for c in copies:
        c.start()
    for c in copies[:4]:
        c.wait()
    leaf = reordered(x[...], p[0, 0:1, :], P1)
    skel = leaf[:S1]
    diff = leaf[S1:] - dot(t[...], skel.astype(BF16))
    z_out[...] = dot(v[...], diff.astype(BF16)).astype(BF16)
    skel_out[...] = skel
    for c in copies[4:]:
        c.wait()


def spread_body(rhs, perm, interp, couple, z, skel0, s0, s1, s2, s3, r1, r2, r3):
    zc = z[...]
    s0[...] = skel0[...] - dot_t(interp[0, 0], zc)
    for n, (s, r) in ((1, (s1, r1)), (2, (s2, r2)), (3, (s3, r3))):
        i, j = BOXES[n]
        leaf = reordered(rhs[i, j], perm[i, j : j + 1, :], P1)
        r[...] = leaf[S1:]
        acc = leaf[:S1]
        for k in range(8):
            if source((i, j), k) == (0, (0, 0)):
                acc = acc - dot_t(couple[i, j, k], zc)
        s[...] = acc


def solve_body(n_ties, box, ks, part, terms, *rest):
    interp, piv, couple, skel, red, *rest = rest[n_ties:]
    zs, rest = rest[: len(ks)], rest[len(ks) :]
    i, j = box
    acc = skel[...]
    if part is not None:
        acc = acc - rest[0][part * S1 : (part + 1) * S1].astype(F32)
        rest = rest[1:]
    for k, z in zip(ks, zs):
        acc = acc - dot_t(couple[i, j, k], z[...])
    diff = red[...] - dot(interp[i, j], acc.astype(BF16))
    z = dot(piv[i, j], diff.astype(BF16)).astype(BF16)
    if terms is None:
        z_out, skel_out = rest
    else:
        left, right, mats, z_out, skel_out, sum_out = rest
        values, at = (left[...], z, right[...]), 0
        for n, (_, ks, which) in enumerate(terms):
            total = None
            for w in which:
                term = dot_t(mats[at], values[w])
                total = term if total is None else total + term
                at += 1
            sum_out[n * S1 : (n + 1) * S1] = total.astype(BF16)
    z_out[...] = z
    skel_out[...] = acc


def update_body(own, jobs, n_z, part, interp, couple, *refs):
    zs, skels, rest = refs[:n_z], refs[n_z : n_z + 4], refs[n_z + 4 :]
    if part is not None:
        arrived, rest = rest[0], rest[1:]
    for n in range(4):
        i, j = BOXES[n]
        acc = skels[n][...]
        if n == own:
            acc = acc - dot_t(interp[i, j], zs[0][...])
        if part == n:
            acc = acc - arrived[S1 : 2 * S1].astype(F32)
        for k, at in jobs[n]:
            acc = acc - dot_t(couple[i, j, k], zs[at][...])
        rest[n][...] = acc


def jobs_of(order, drop=()):
    jobs = [[], [], [], []]
    for n in range(4):
        for k in range(8):
            where = source(BOXES[n], k)
            if where in order and (n, where) not in drop:
                jobs[n].append((k, order.index(where)))
    return jobs


def work(rhs, perm1, interp1, pivinv1, couple1, perm2, interp2, pivinv2, couple2):
    couple1 = couple1.swapaxes(3, 4)
    have = {}
    here = (0, 0)

    def solve(colour, keys, skels, reds, arrived=None, part=None, terms=None, extra=(), ties=()):
        box = BOXES[colour]
        ks, zs = [], []
        for k in range(8):
            if source(box, k) in keys:
                ks.append(k)
                zs.append(have[source(box, k)])
        ins = [interp1, pivinv1, couple1, skels[colour], reds[colour], *zs]
        if arrived is not None:
            ins.append(arrived)
        outs = [LEAF_Z, LEAF_S] + ([LEAF_M] if terms else [])
        body = functools.partial(solve_body, len(ties), box, ks, part, terms)
        out = call(body, [*ties, *ins, *extra], outs, specs=[ANY] * len(ties))
        have[(colour, here)] = out[0]
        skels = list(skels)
        skels[colour] = out[1]
        return out[0], skels, out[2:]

    def update(own, keys, skels, drop=(), arrived=None, part=None):
        order = [(own, here), *keys]
        ins = [interp1, couple1, *[have[key] for key in order], *skels] + ([arrived] if arrived is not None else [])
        body = functools.partial(update_body, own, jobs_of(order, drop), len(order), part)
        return call(body, ins, [LEAF_S] * 4)

    dma = pltpu.SemaphoreType.DMA((4 + 4 + 6,))
    z00, skel0, up_pack, down_pack, *packs = call(
        first_body,
        [pltpu.with_memory_space_constraint(x, pltpu.HBM) for x in (rhs, perm1, interp1, pivinv1, couple1, couple2)],
        [LEAF_Z, LEAF_S, LEAF_W, LEAF_W] + [((n, S2, R2), BF16) for _, n, _ in PACKS.values()],
        specs=[HBM] * 6,
        scratch=[
            pltpu.VMEM((P1, K), F32),
            pltpu.VMEM((2, 2, P1), jnp.int32),
            pltpu.VMEM((R1, S1), BF16),
            pltpu.VMEM((R1, R1), BF16),
            dma,
        ],
    )
    packs = dict(zip(PACKS, packs))
    have[(0, here)] = z00
    have[(0, (0, 1))] = shift(z00, (0, -1))
    up_mats = shift(up_pack, (1, 0))
    down_mats = shift(down_pack, (-1, 0))
    s0, s1, s2, s3, r1, r2, r3 = call(
        spread_body, [rhs, perm1, interp1, couple1, z00, skel0], [LEAF_S] * 4 + [LEAF_R] * 3
    )
    reds = [None, r1, r2, r3]
    z01, skels, (up_sum,) = solve(
        1, {(0, (0, 1))}, [s0, s1, s2, s3], reds, terms=UP_TERMS, extra=(z00, have[(0, (0, 1))], up_mats), ties=(down_mats,)
    )
    from_below = shift(up_sum, (-1, 0))
    have[(1, (1, -1))] = shift(z01, (-1, 1))
    have[(1, (0, -1))] = shift(z01, (0, 1))
    mats = {}

    def fetch(dx, value):
        (ready, value) = after([packs[to] for to in PACKS if to[0] == dx], value)
        for to, pack in zip([to for to in PACKS if to[0] == dx], ready):
            mats[(-to[0], -to[1])] = shift(pack, to, (1, 3) if to[1] == 0 else (0, 2))
        return value, [mats[(-to[0], -to[1])] for to in PACKS if to[0] == dx]

    z01, fetched = fetch(1, z01)
    have[(1, here)] = z01
    skels = update(1, [(0, (0, 1))], skels, drop=[(1, (0, (0, 1)))])
    z10, skels, _ = solve(2, {(1, (0, -1)), (1, (1, -1))}, skels, reds, arrived=from_below, part=0, ties=fetched)
    have[(2, (0, 1))] = shift(z10, (0, -1))
    z10, fetched = fetch(-1, z10)
    have[(2, here)] = z10
    skels = update(2, [(1, (0, -1))], skels, drop=[(2, (1, (0, -1)))], arrived=from_below, part=3)
    z11, skels, (down_sum,) = solve(
        3, {(2, (0, 1))}, skels, reds, terms=DOWN_TERMS, extra=(z10, have[(2, (0, 1))], down_mats), ties=fetched
    )
    from_above = shift(down_sum, (1, 0))
    have[(3, (-1, -1))] = shift(z11, (1, 1))
    have[(3, (0, -1))] = shift(z11, (0, 1))
    skels = update(3, [(2, (0, 1))], skels, drop=[(3, (2, (0, 1)))])
    red1 = jnp.stack([z00, z01, z10, z11]).reshape(2, 2, R1, K)

    colour = ((lax.axis_index("bx") % 2) * 2 + lax.axis_index("by") % 2).astype(jnp.int32).reshape(1)
    last = [(3, (0, -1)), (3, (-1, -1))]
    last_jobs = jobs_of(last)

    def solve_parent(interp, piv, skel, red):
        diff = red - dot(interp[0, 0], skel.astype(BF16))
        return dot(piv[0, 0], diff.astype(BF16)).astype(BF16)

    def join_body(me, perm, interp, piv, couple, za, zb, arrived, ca, cb, cc, cd, skel_out, red_out, z_out):
        zs = [za, zb]
        parts = []
        for n, c in enumerate((ca, cb, cc, cd)):
            acc = c[...]
            if n < 2:
                acc = acc - arrived[n * S1 : (n + 1) * S1].astype(F32)
            for k, at in last_jobs[n]:
                acc = acc - dot_t(couple[BOXES[n][0], BOXES[n][1], k], zs[at][...])
            parts.append(acc)
        parent = reordered(jnp.concatenate(parts, axis=0), perm[0], P2)
        skel_out[...] = parent[:S2]
        red_out[...] = parent[S2:]

        @pl.when(me[0] == 0)
        def _():
            z_out[...] = solve_parent(interp, piv, parent[:S2], parent[S2:])

    skel, red, z0 = call(
        join_body,
        [colour, perm2, interp2, pivinv2, couple1, *[have[key] for key in last], from_above, *skels],
        [PAR_S, PAR_R, PAR_Z],
        specs=[SMEM],
    )

    def sides(z, c):
        return shift(z, (0, 1), (c,)), shift(z, (0, -1), (c,))

    def odd_body(c, me, interp, piv, couple, skel, red, zl, zr, *rest):
        if c == 3:
            arrived, rest = rest[:2], rest[2:]
        ws, (z_out, skel_out), sums = rest[:6], rest[6:8], rest[8:]

        @pl.when(me[0] != c)
        def _():
            skel_out[...] = skel[...]

        @pl.when(me[0] == c)
        def _():
            acc = skel[...]
            if c == 3:
                acc = acc - arrived[0][...].astype(F32) - arrived[1][...].astype(F32)
            acc = acc - (dot(couple[0, 0, 3], zl[...]) + dot(couple[0, 0, 4], zr[...]))
            skel_out[...] = acc
            z = solve_parent(interp, piv, acc, red[...])
            z_out[...] = z
            values = (zl[...], z, zr[...])
            for (_, _, which), w, out in zip(PACKS.values(), ws, sums):
                total = None
                for n, v in enumerate(which):
                    term = dot(w[n], values[v])
                    total = term if total is None else total + term
                out[...] = total.astype(BF16)

    def odd(c, skel, zl, zr, arrived=()):
        ws = [mats[(-dx, -dy)] for dx, dy in PACKS]
        z, skel, *sums = call(
            functools.partial(odd_body, c),
            [colour, interp2, pivinv2, couple2, skel, red, zl, zr, *arrived, *ws],
            [PAR_Z, PAR_S] + [PAR_M] * 6,
            specs=[SMEM],
        )
        got = {}
        for way in CORNERS + ENDS:
            got[way] = shift(sums[list(PACKS).index((-way[0], -way[1]))], way, (c,))
        return z, skel, got

    def even_body(me, interp, piv, skel, red, a, b, c, d, z_out, skel_out):
        @pl.when(me[0] != 2)
        def _():
            skel_out[...] = skel[...]

        @pl.when(me[0] == 2)
        def _():
            acc = skel[...] - (a[...].astype(F32) + b[...].astype(F32) + c[...].astype(F32) + d[...].astype(F32))
            skel_out[...] = acc
            z_out[...] = solve_parent(interp, piv, acc, red[...])

    zl, zr = sides(z0, 0)
    z1, skel, got1 = odd(1, skel, zl, zr)
    side1 = sides(z1, 1)
    z2, skel = call(
        even_body, [colour, interp2, pivinv2, skel, red, *[got1[way] for way in CORNERS]], [PAR_Z, PAR_S], specs=[SMEM]
    )
    zl, zr = sides(z2, 2)
    z3, skel, got3 = odd(3, skel, zl, zr, [got1[way] for way in ENDS])
    side3 = sides(z3, 3)

    def early_body(me, interp, couple, skel, z0, z1, z2, z3, xl, xr, skel_out, z_out):
        for c, own in enumerate((z0, z1, z2, z3)):

            @pl.when(me[0] == c)
            def _():
                zc = own[...]
                z_out[...] = zc
                acc = skel[...] - dot_t(interp[0, 0], zc)
                if c == 0:
                    acc = acc - (dot(couple[0, 0, 3], xl[...]) + dot(couple[0, 0, 4], xr[...]))
                skel_out[...] = acc

    skel, red2 = call(
        early_body, [colour, interp2, couple2, skel, z0, z1, z2, z3, *side1], [PAR_S, PAR_Z], specs=[SMEM]
    )

    def late_body(me, couple, skel, a, b, c, d, e, f, xl, xr, skel_out):
        @pl.when(me[0] == 0)
        def _():
            skel_out[...] = skel[...] - (
                a[...].astype(F32) + b[...].astype(F32) + c[...].astype(F32) + d[...].astype(F32)
            )

        @pl.when(me[0] == 1)
        def _():
            skel_out[...] = skel[...] - (e[...].astype(F32) + f[...].astype(F32))

        @pl.when(me[0] == 2)
        def _():
            skel_out[...] = skel[...] - (dot(couple[0, 0, 3], xl[...]) + dot(couple[0, 0, 4], xr[...]))

        @pl.when(me[0] == 3)
        def _():
            skel_out[...] = skel[...]

    (skel2,) = call(
        late_body, [colour, couple2, skel, *[got3[way] for way in CORNERS + ENDS], *side3], [PAR_S], specs=[SMEM]
    )
    return (red1, red2[None, None], skel2[None, None])


def solution(mesh):
    in_specs = (
        P("bx", "by", None, None),
        P("bx", "by", None),
        P("bx", "by", None, None),
        P("bx", "by", None, None),
        P("bx", "by", None, None, None),
        P("bx", "by", None),
        P("bx", "by", None, None),
        P("bx", "by", None, None),
        P("bx", "by", None, None, None),
    )
    out_specs = (P("bx", "by", None, None), P("bx", "by", None, None), P("bx", "by", None, None))
    return jax.shard_map(work, mesh=mesh, in_specs=in_specs, out_specs=out_specs, check_vma=False)
```

```python
import functools

import jax
import jax.numpy as jnp
from jax import lax
from jax.experimental import pallas as pl
from jax.experimental.pallas import tpu as pltpu
from jax.sharding import PartitionSpec as P


S1, R1, P1 = 96, 160, 256
S2, R2, P2 = 128, 256, 384
K = 384
OFFSETS = [(-1, -1), (-1, 0), (-1, 1), (0, -1), (0, 1), (1, -1), (1, 0), (1, 1)]
BOXES = [(0, 0), (0, 1), (1, 0), (1, 1)]
F32, BF16 = jnp.float32, jnp.bfloat16
LEAF_S, LEAF_R, LEAF_Z = ((4, S1, K), F32), ((3, R1, K), F32), ((R1, K), BF16)
LEAF_W, LEAF_M = ((5, R1, S1), BF16), ((2 * S1, K), BF16)
PAR_W = ((3, S2, R2), BF16)
PAR_S, PAR_R, PAR_Z, PAR_M = ((S2, K), F32), ((R2, K), F32), ((R2, K), BF16), ((S2, K), BF16)


UP_TERMS = [((1, 0), (6, 7)), ((1, 1), (5, 6, 7))]
DOWN_TERMS = [((0, 0), (1, 2)), ((0, 1), (0, 1, 2))]


def dot(a, b):
    return lax.dot_general(a, b, (((1,), (0,)), ((), ())), preferred_element_type=F32)


def dot_t(a, b):
    return lax.dot_general(a, b, (((0,), (0,)), ((), ())), preferred_element_type=F32)


def source(box, k):
    row, col = box[0] + OFFSETS[k][0], box[1] + OFFSETS[k][1]
    return (row % 2) * 2 + col % 2, (row // 2, col // 2)


def reordered(x, perm, rows):
    pick = (lax.broadcasted_iota(jnp.int32, (rows, rows), 0) == perm).astype(F32).astype(BF16)
    high = x.astype(BF16)
    low = (x - high.astype(F32)).astype(BF16)
    return dot_t(pick, high) + dot_t(pick, low)


SMEM, VMEM, HBM = (pl.BlockSpec(memory_space=s) for s in (pltpu.SMEM, pltpu.VMEM, pltpu.HBM))


def call(body, ins, outs, specs=(), scratch=(), alias=None):
    specs = list(specs) + [VMEM] * (len(ins) - len(specs))
    return pl.pallas_call(
        body,
        out_shape=[jax.ShapeDtypeStruct(s, d) for s, d in outs],
        in_specs=specs,
        out_specs=[VMEM] * len(outs),
        scratch_shapes=list(scratch),
        input_output_aliases=alias or {},
        compiler_params=pltpu.CompilerParams(vmem_limit_bytes=20 * 1024 * 1024),
        cost_estimate=pl.CostEstimate(flops=300_000_000, bytes_accessed=2_000_000, transcendentals=0),
    )(*ins)


def pairs(dx, dy, colours):
    nx, ny = lax.axis_size("bx"), lax.axis_size("by")
    out = []
    for i in range(nx):
        for j in range(ny):
            if (i % 2) * 2 + j % 2 in colours and 0 <= i + dx < nx and 0 <= j + dy < ny:
                out.append((i * ny + j, (i + dx) * ny + j + dy))
    return out


def shift(x, to, colours=(0, 1, 2, 3)):
    return lax.ppermute(x, ("bx", "by"), pairs(*to, colours))


def after(x, value):
    return lax.optimization_barrier((x, value))


def first_body(rhs, perm, interp, piv, couple, top, z_out, skel_out, up_out, down_out, below_out, above_out, *rest):
    x, p, t, v, sems = rest
    jobs = [(rhs.at[0, 0], x), (perm, p), (interp.at[0, 0], t), (piv.at[0, 0], v)]
    for terms, out in ((UP_TERMS, up_out), (DOWN_TERMS, down_out)):
        at = 0
        for (i, j), ks in terms:
            jobs.append((couple.at[i, j, pl.ds(ks[0], len(ks))], out.at[pl.ds(at, len(ks))]))
            at += len(ks)
    jobs.append((top.at[0, 0, pl.ds(5, 3)], below_out))
    jobs.append((top.at[0, 0, pl.ds(0, 3)], above_out))
    copies = [pltpu.make_async_copy(a, b, sems.at[n]) for n, (a, b) in enumerate(jobs)]
    for c in copies:
        c.start()
    for c in copies[:4]:
        c.wait()
    leaf = reordered(x[...], p[0, 0:1, :], P1)
    skel = leaf[:S1]
    diff = leaf[S1:] - dot(t[...], skel.astype(BF16))
    z_out[...] = dot(v[...], diff.astype(BF16)).astype(BF16)
    skel_out[...] = skel
    for c in copies[4:]:
        c.wait()


def spread_body(rhs, perm, interp, couple, z, skel0, skels, reds):
    zc = z[...]
    skels[0] = skel0[...] - dot_t(interp[0, 0], zc)
    for n in (1, 2, 3):
        i, j = BOXES[n]
        leaf = reordered(rhs[i, j], perm[i, j : j + 1, :], P1)
        reds[n - 1] = leaf[S1:]
        acc = leaf[:S1]
        for k in range(8):
            if source((i, j), k) == (0, (0, 0)):
                acc = acc - dot_t(couple[i, j, k], zc)
        skels[n] = acc


def solve_body(colour, ks, part, interp, piv, couple, skels, reds, *rest):
    zs, (*arrived, z_out, out) = rest[: len(ks)], rest[len(ks) :]
    i, j = BOXES[colour]
    acc = skels[colour]
    if part is not None:
        acc = acc - arrived[0][part * S1 : (part + 1) * S1].astype(F32)
    for k, z in zip(ks, zs):
        acc = acc - dot_t(couple[i, j, k], z[...])
    diff = reds[colour - 1] - dot(interp[i, j], acc.astype(BF16))
    z_out[...] = dot(piv[i, j], diff.astype(BF16)).astype(BF16)
    out[...] = skels[...]
    out[colour] = acc


def sum_body(terms, left, own, right, mats, out):
    values, at = (left[...], own[...], right[...]), 0
    for n, (_, ks) in enumerate(terms):
        total = None
        for w in range(len(ks)):
            term = dot_t(mats[at], values[w])
            total = term if total is None else total + term
            at += 1
        out[n * S1 : (n + 1) * S1] = total.astype(BF16)


def update_body(own, jobs, n_z, part, interp, couple, *refs):
    zs, (skels, *arrived, out) = refs[:n_z], refs[n_z:]
    for n in range(4):
        i, j = BOXES[n]
        acc = skels[n]
        if n == own:
            acc = acc - dot_t(interp[i, j], zs[0][...])
        if part == n:
            acc = acc - arrived[0][S1 : 2 * S1].astype(F32)
        for k, at in jobs[n]:
            acc = acc - dot_t(couple[i, j, k], zs[at][...])
        out[n] = acc


def pick_body(perm, pick_out):
    hit = (lax.broadcasted_iota(jnp.int32, (P2, P2), 0) == perm[0]).astype(F32)
    pick_out[...] = hit.T.astype(BF16)


def jobs_of(order, drop=()):
    jobs = [[], [], [], []]
    for n in range(4):
        for k in range(8):
            where = source(BOXES[n], k)
            if where in order and (n, where) not in drop:
                jobs[n].append((k, order.index(where)))
    return jobs


def work(rhs, perm1, interp1, pivinv1, couple1, perm2, interp2, pivinv2, couple2):
    couple1 = couple1.swapaxes(3, 4)
    have = {}
    here = (0, 0)

    def solve(colour, keys, skels, reds, arrived=None, part=None):
        box = BOXES[colour]
        ks, zs = [], []
        for k in range(8):
            if source(box, k) in keys:
                ks.append(k)
                zs.append(have[source(box, k)])
        ins = [interp1, pivinv1, couple1, skels, reds, *zs] + ([arrived] if arrived is not None else [])
        body = functools.partial(solve_body, colour, ks, part)
        z, skels = call(body, ins, [LEAF_Z, LEAF_S])
        have[(colour, here)] = z
        return z, skels

    def total(terms, left, own, right, mats):
        return call(functools.partial(sum_body, terms), [left, own, right, mats], [LEAF_M])[0]

    def update(own, keys, skels, drop=(), arrived=None, part=None):
        order = [(own, here), *keys]
        ins = [interp1, couple1, *[have[key] for key in order], skels] + ([arrived] if arrived is not None else [])
        body = functools.partial(update_body, own, jobs_of(order, drop), len(order), part)
        return call(body, ins, [LEAF_S])[0]

    z00, skel0, up_pack, down_pack, below_pack, above_pack = call(
        first_body,
        [pltpu.with_memory_space_constraint(x, pltpu.HBM) for x in (rhs, perm1, interp1, pivinv1, couple1, couple2)],
        [LEAF_Z, ((S1, K), F32), LEAF_W, LEAF_W, PAR_W, PAR_W],
        specs=[HBM] * 6,
        scratch=[
            pltpu.VMEM((P1, K), F32),
            pltpu.VMEM((2, 2, P1), jnp.int32),
            pltpu.VMEM((R1, S1), BF16),
            pltpu.VMEM((R1, R1), BF16),
            pltpu.SemaphoreType.DMA((4 + 4 + 2,)),
        ],
    )
    have[(0, here)] = z00
    z00r = have[(0, (0, 1))] = shift(z00, (0, -1))
    up_mats = shift(up_pack, (1, 0))
    skels, reds = call(spread_body, [rhs, perm1, interp1, couple1, z00, skel0], [LEAF_S, LEAF_R])
    z01, skels = solve(1, {(0, (0, 1))}, skels, reds)
    have[(1, (1, -1))] = shift(z01, (-1, 1))
    from_below = shift(total(UP_TERMS, z00, z01, z00r, up_mats), (-1, 0))
    have[(1, (0, -1))] = shift(z01, (0, 1))
    below_pack, z01 = after(below_pack, z01)
    have[(1, here)] = z01
    above_mats = shift(below_pack, (1, 0))
    skels = update(1, [(0, (0, 1))], skels, drop=[(1, (0, (0, 1)))])
    z10, skels = solve(2, {(1, (0, -1)), (1, (1, -1))}, skels, reds, arrived=from_below, part=0)
    z10r = have[(2, (0, 1))] = shift(z10, (0, -1))
    down_pack, z10 = after(down_pack, z10)
    have[(2, here)] = z10
    down_mats = shift(down_pack, (-1, 0))
    skels = update(2, [(1, (0, -1))], skels, drop=[(2, (1, (0, -1)))], arrived=from_below, part=3)
    z11, skels = solve(3, {(2, (0, 1))}, skels, reds)
    have[(3, (-1, -1))] = shift(z11, (1, 1))
    from_above = shift(total(DOWN_TERMS, z10, z11, z10r, down_mats), (1, 0))
    have[(3, (0, -1))] = shift(z11, (0, 1))
    above_pack, z11 = after(above_pack, z11)
    have[(3, here)] = z11
    below_mats = shift(above_pack, (-1, 0))
    skels = update(3, [(2, (0, 1))], skels, drop=[(3, (2, (0, 1)))])
    (pick,) = call(pick_body, [perm2], [((P2, P2), BF16)])
    red1 = jnp.stack([z00, z01, z10, z11]).reshape(2, 2, R1, K)

    colour = ((lax.axis_index("bx") % 2) * 2 + lax.axis_index("by") % 2).astype(jnp.int32).reshape(1)
    last = [(3, (0, -1)), (3, (-1, -1))]
    last_jobs = jobs_of(last)

    def solve_parent(interp, piv, skel, red):
        diff = red - dot(interp[0, 0], skel.astype(BF16))
        return dot(piv[0, 0], diff.astype(BF16)).astype(BF16)

    def join_body(me, pick, interp, piv, couple, za, zb, arrived, children, skel_out, red_out, z_out):
        zs = [za, zb]
        parts = []
        for n in range(4):
            acc = children[n]
            if n < 2:
                acc = acc - arrived[n * S1 : (n + 1) * S1].astype(F32)
            for k, at in last_jobs[n]:
                acc = acc - dot_t(couple[BOXES[n][0], BOXES[n][1], k], zs[at][...])
            parts.append(acc)
        x = jnp.concatenate(parts, axis=0)
        high = x.astype(BF16)
        low = (x - high.astype(F32)).astype(BF16)
        parent = dot(pick[...], high) + dot(pick[...], low)
        skel_out[...] = parent[:S2]
        red_out[...] = parent[S2:]

        @pl.when(me[0] == 0)
        def _():
            z_out[...] = solve_parent(interp, piv, parent[:S2], parent[S2:])

    skel, red, z0 = call(
        join_body,
        [colour, pick, interp2, pivinv2, couple1, *[have[key] for key in last], from_above, skels],
        [PAR_S, PAR_R, PAR_Z],
        specs=[SMEM],
    )

    def sides(z, c):
        return shift(z, (0, 1), (c,)), shift(z, (0, -1), (c,))

    def ends(sums, row):
        colours = (2 * row, 2 * row + 1)
        return shift(sums[0], (-1, 0), colours), shift(sums[1], (1, 0), colours)

    def parent_body(c, me, interp, piv, couple, skel, red, *rest):
        *got, z_out, skel_out = rest

        @pl.when(me[0] != c)
        def _():
            skel_out[...] = skel[...]

        @pl.when(me[0] == c)
        def _():
            acc = skel[...]
            if c % 2:
                acc = acc - (dot(couple[0, 0, 3], got[0][...]) + dot(couple[0, 0, 4], got[1][...]))
            if c >= 2:
                acc = acc - (got[-2][...].astype(F32) + got[-1][...].astype(F32))
            skel_out[...] = acc
            z_out[...] = solve_parent(interp, piv, acc, red[...])

    def parent(c, skel, got):
        return call(
            functools.partial(parent_body, c),
            [colour, interp2, pivinv2, couple2, skel, red, *got],
            [PAR_Z, PAR_S],
            specs=[SMEM],
        )

    def row_body(row, me, above, below, el, er, ol, orr, ze, zo, up_out, down_out):
        for c, (a, own, b) in ((2 * row, (ol, ze, orr)), (2 * row + 1, (el, zo, er))):

            @pl.when(me[0] == c)
            def _():
                for w, out in ((above, up_out), (below, down_out)):
                    total = dot(w[0], a[...]) + dot(w[1], own[...]) + dot(w[2], b[...])
                    out[...] = total.astype(BF16)

    def row(n, even, odd, z_even, z_odd):
        return call(
            functools.partial(row_body, n),
            [colour, above_mats, below_mats, *even, *odd, z_even, z_odd],
            [PAR_M, PAR_M],
            specs=[SMEM],
        )

    side0 = sides(z0, 0)
    z1, skel = parent(1, skel, side0)
    side1 = sides(z1, 1)
    end0 = ends(row(0, side0, side1, z0, z1), 0)
    z2, skel = parent(2, skel, end0)
    side2 = sides(z2, 2)
    z3, skel = parent(3, skel, (*side2, *end0))
    side3 = sides(z3, 3)
    end1 = ends(row(1, side2, side3, z2, z3), 1)

    def early_body(me, interp, couple, skel, z0, z1, z2, z3, al, ar, bl, br, skel_out, z_out):
        for c, own in enumerate((z0, z1, z2, z3)):

            @pl.when(me[0] == c)
            def _():
                zc = own[...]
                z_out[...] = zc
                acc = skel[...] - dot_t(interp[0, 0], zc)
                if c % 2 == 0:
                    xl, xr = ((al, ar), (bl, br))[c // 2]
                    acc = acc - (dot(couple[0, 0, 3], xl[...]) + dot(couple[0, 0, 4], xr[...]))
                skel_out[...] = acc

    skel, red2 = call(
        early_body, [colour, interp2, couple2, skel, z0, z1, z2, z3, *side1, *side3], [PAR_S, PAR_Z], specs=[SMEM]
    )

    def late_body(me, skel, a, b, skel_out):
        @pl.when(me[0] < 2)
        def _():
            skel_out[...] = skel[...] - (a[...].astype(F32) + b[...].astype(F32))

        @pl.when(me[0] >= 2)
        def _():
            skel_out[...] = skel[...]

    (skel2,) = call(late_body, [colour, skel, *end1], [PAR_S], specs=[SMEM])
    return (red1, red2[None, None], skel2[None, None])


def solution(mesh):
    in_specs = (
        P("bx", "by", None, None),
        P("bx", "by", None),
        P("bx", "by", None, None),
        P("bx", "by", None, None),
        P("bx", "by", None, None, None),
        P("bx", "by", None),
        P("bx", "by", None, None),
        P("bx", "by", None, None),
        P("bx", "by", None, None, None),
    )
    out_specs = (P("bx", "by", None, None), P("bx", "by", None, None), P("bx", "by", None, None))
    return jax.shard_map(work, mesh=mesh, in_specs=in_specs, out_specs=out_specs, check_vma=False)
```

```python
import functools

import jax
import jax.numpy as jnp
from jax import lax
from jax.experimental import pallas as pl
from jax.experimental.pallas import tpu as pltpu
from jax.sharding import PartitionSpec as P


S1, R1, P1 = 96, 160, 256
S2, R2, P2 = 128, 256, 384
K = 384
OFFSETS = [(-1, -1), (-1, 0), (-1, 1), (0, -1), (0, 1), (1, -1), (1, 0), (1, 1)]
BOXES = [(0, 0), (0, 1), (1, 0), (1, 1)]
F32, BF16 = jnp.float32, jnp.bfloat16
LEAF_S, LEAF_R, LEAF_Z = ((4, S1, K), F32), ((3, R1, K), F32), ((R1, K), BF16)
LEAF_W, LEAF_M = ((5, R1, S1), BF16), ((2 * S1, K), BF16)
PAR_W = ((3, S2, R2), BF16)
PAR_S, PAR_R, PAR_Z, PAR_M = ((S2, K), F32), ((R2, K), F32), ((R2, K), BF16), ((S2, K), BF16)


DOWN_TERMS = [((0, 0), (1, 2)), ((0, 1), (0, 1, 2))]


def dot(a, b):
    return lax.dot_general(a, b, (((1,), (0,)), ((), ())), preferred_element_type=F32)


def dot_t(a, b):
    return lax.dot_general(a, b, (((0,), (0,)), ((), ())), preferred_element_type=F32)


def source(box, k):
    row, col = box[0] + OFFSETS[k][0], box[1] + OFFSETS[k][1]
    return (row % 2) * 2 + col % 2, (row // 2, col // 2)


def reordered(x, perm, rows):
    pick = (lax.broadcasted_iota(jnp.int32, (rows, rows), 0) == perm).astype(F32).astype(BF16)
    high = x.astype(BF16)
    low = (x - high.astype(F32)).astype(BF16)
    return dot_t(pick, high) + dot_t(pick, low)


SMEM, VMEM, ANY, HBM = (pl.BlockSpec(memory_space=s) for s in (pltpu.SMEM, pltpu.VMEM, pl.ANY, pltpu.HBM))


def call(body, ins, outs, specs=(), scratch=(), alias=None):
    specs = list(specs) + [VMEM] * (len(ins) - len(specs))
    return pl.pallas_call(
        body,
        out_shape=[jax.ShapeDtypeStruct(s, d) for s, d in outs],
        in_specs=specs,
        out_specs=[VMEM] * len(outs),
        scratch_shapes=list(scratch),
        input_output_aliases=alias or {},
        compiler_params=pltpu.CompilerParams(vmem_limit_bytes=20 * 1024 * 1024),
        cost_estimate=pl.CostEstimate(flops=300_000_000, bytes_accessed=2_000_000, transcendentals=0),
    )(*ins)


def pairs(dx, dy, colours):
    nx, ny = lax.axis_size("bx"), lax.axis_size("by")
    out = []
    for i in range(nx):
        for j in range(ny):
            if (i % 2) * 2 + j % 2 in colours and 0 <= i + dx < nx and 0 <= j + dy < ny:
                out.append((i * ny + j, (i + dx) * ny + j + dy))
    return out


def shift(x, to, colours=(0, 1, 2, 3)):
    return lax.ppermute(x, ("bx", "by"), pairs(*to, colours))


def after(x, value):
    return lax.optimization_barrier((x, value))


def first_body(rhs, perm, interp, piv, z_out, skel_out, x, p, t, v, sems):
    jobs = [(rhs.at[0, 0], x), (perm, p), (interp.at[0, 0], t), (piv.at[0, 0], v)]
    copies = [pltpu.make_async_copy(a, b, sems.at[n]) for n, (a, b) in enumerate(jobs)]
    for c in copies:
        c.start()
    for c in copies:
        c.wait()
    leaf = reordered(x[...], p[0, 0:1, :], P1)
    skel = leaf[:S1]
    diff = leaf[S1:] - dot(t[...], skel.astype(BF16))
    z_out[...] = dot(v[...], diff.astype(BF16)).astype(BF16)
    skel_out[...] = skel


def pack_body(couple, top, tie, down_out, below_out, above_out, sems):
    jobs, at = [(top.at[0, 0, pl.ds(5, 3)], below_out), (top.at[0, 0, pl.ds(0, 3)], above_out)], 0
    for (i, j), ks in DOWN_TERMS:
        jobs.append((couple.at[i, j, pl.ds(ks[0], len(ks))], down_out.at[pl.ds(at, len(ks))]))
        at += len(ks)
    copies = [pltpu.make_async_copy(a, b, sems.at[n]) for n, (a, b) in enumerate(jobs)]
    for c in copies:
        c.start()
    for c in copies:
        c.wait()


def spread_body(rhs, perm, interp, couple, z, skel0, skels, reds):
    zc = z[...]
    skels[0] = skel0[...] - dot_t(interp[0, 0], zc)
    for n in (1, 2, 3):
        i, j = BOXES[n]
        leaf = reordered(rhs[i, j], perm[i, j : j + 1, :], P1)
        reds[n - 1] = leaf[S1:]
        acc = leaf[:S1]
        for k in range(8):
            if source((i, j), k) == (0, (0, 0)):
                acc = acc - dot_t(couple[i, j, k], zc)
        skels[n] = acc


def solve_body(colour, ks, interp, piv, couple, skels, reds, *rest):
    *zs, z_out, out = rest
    i, j = BOXES[colour]
    acc = skels[colour]
    for k, z in zip(ks, zs):
        acc = acc - dot_t(couple[i, j, k], z[...])
    diff = reds[colour - 1] - dot(interp[i, j], acc.astype(BF16))
    z_out[...] = dot(piv[i, j], diff.astype(BF16)).astype(BF16)
    out[...] = skels[...]
    out[colour] = acc


def sum_body(terms, left, own, right, mats, out):
    values, at = (left[...], own[...], right[...]), 0
    for n, (_, ks) in enumerate(terms):
        total = None
        for w in range(len(ks)):
            term = dot_t(mats[at], values[w])
            total = term if total is None else total + term
            at += 1
        out[n * S1 : (n + 1) * S1] = total.astype(BF16)


def update_body(own, jobs, n_z, interp, couple, *refs):
    zs, (skels, out) = refs[:n_z], refs[n_z:]
    for n in range(4):
        i, j = BOXES[n]
        acc = skels[n]
        if n == own:
            acc = acc - dot_t(interp[i, j], zs[0][...])
        for k, at in jobs[n]:
            acc = acc - dot_t(couple[i, j, k], zs[at][...])
        out[n] = acc


def pick_body(perm, pick_out):
    hit = (lax.broadcasted_iota(jnp.int32, (P2, P2), 0) == perm[0]).astype(F32)
    pick_out[...] = hit.T.astype(BF16)


def jobs_of(order, drop=()):
    jobs = [[], [], [], []]
    for n in range(4):
        for k in range(8):
            where = source(BOXES[n], k)
            if where in order and (n, where) not in drop:
                jobs[n].append((k, order.index(where)))
    return jobs


def work(rhs, perm1, interp1, pivinv1, couple1, perm2, interp2, pivinv2, couple2):
    couple1 = couple1.swapaxes(3, 4)
    have = {}
    here = (0, 0)

    def solve(colour, keys, skels, reds):
        box = BOXES[colour]
        ks, zs = [], []
        for k in range(8):
            if source(box, k) in keys:
                ks.append(k)
                zs.append(have[source(box, k)])
        body = functools.partial(solve_body, colour, ks)
        z, skels = call(body, [interp1, pivinv1, couple1, skels, reds, *zs], [LEAF_Z, LEAF_S])
        have[(colour, here)] = z
        return z, skels

    def total(terms, left, own, right, mats):
        return call(functools.partial(sum_body, terms), [left, own, right, mats], [LEAF_M])[0]

    def update(own, keys, skels, drop=()):
        order = [(own, here), *keys]
        body = functools.partial(update_body, own, jobs_of(order, drop), len(order))
        return call(body, [interp1, couple1, *[have[key] for key in order], skels], [LEAF_S])[0]

    z00, skel0 = call(
        first_body,
        [pltpu.with_memory_space_constraint(x, pltpu.HBM) for x in (rhs, perm1, interp1, pivinv1)],
        [LEAF_Z, ((S1, K), F32)],
        specs=[HBM] * 4,
        scratch=[
            pltpu.VMEM((P1, K), F32),
            pltpu.VMEM((2, 2, P1), jnp.int32),
            pltpu.VMEM((R1, S1), BF16),
            pltpu.VMEM((R1, R1), BF16),
            pltpu.SemaphoreType.DMA((4,)),
        ],
    )
    have[(0, here)] = z00
    have[(0, (0, 1))] = shift(z00, (0, -1))
    have[(0, (1, 0))] = shift(z00, (-1, 0))
    down_pack, below_pack, above_pack = call(
        pack_body,
        [*[pltpu.with_memory_space_constraint(x, pltpu.HBM) for x in (couple1, couple2)], z00],
        [LEAF_W, PAR_W, PAR_W],
        specs=[HBM, HBM, ANY],
        scratch=[pltpu.SemaphoreType.DMA((4,))],
    )
    down_mats = shift(down_pack, (-1, 0))
    skels, reds = call(spread_body, [rhs, perm1, interp1, couple1, z00, skel0], [LEAF_S, LEAF_R])
    z01, skels = solve(1, {(0, (0, 1))}, skels, reds)
    have[(1, (1, 0))] = shift(z01, (-1, 0))
    have[(1, (1, -1))] = shift(z01, (-1, 1))
    have[(1, (0, -1))] = shift(z01, (0, 1))
    skels = update(1, [(0, (0, 1))], skels, drop=[(1, (0, (0, 1)))])
    below = [(1, (0, -1)), (1, (1, 0)), (0, (1, 0))]
    z10, skels = solve(2, {*below, (1, (1, -1))}, skels, reds)
    z10r = have[(2, (0, 1))] = shift(z10, (0, -1))
    have[(0, (1, 1))] = shift(z00, (-1, -1))
    skels = update(2, below, skels, drop=[(2, key) for key in below])
    z11, skels = solve(3, {(2, (0, 1)), (0, (1, 1))}, skels, reds)
    have[(3, (-1, -1))] = shift(z11, (1, 1))
    from_above = shift(total(DOWN_TERMS, z10, z11, z10r, down_mats), (1, 0))
    have[(3, (0, -1))] = shift(z11, (0, 1))
    skels = update(3, [(2, (0, 1))], skels, drop=[(3, (2, (0, 1)))])
    (pick,) = call(pick_body, [perm2], [((P2, P2), BF16)])
    red1 = jnp.stack([z00, z01, z10, z11]).reshape(2, 2, R1, K)

    colour = ((lax.axis_index("bx") % 2) * 2 + lax.axis_index("by") % 2).astype(jnp.int32).reshape(1)
    last = [(3, (0, -1)), (3, (-1, -1))]
    last_jobs = jobs_of(last)

    def solve_parent(interp, piv, skel, red):
        diff = red - dot(interp[0, 0], skel.astype(BF16))
        return dot(piv[0, 0], diff.astype(BF16)).astype(BF16)

    def join_body(me, pick, interp, piv, couple, za, zb, arrived, children, skel_out, red_out, z_out):
        zs = [za, zb]
        parts = []
        for n in range(4):
            acc = children[n]
            if n < 2:
                acc = acc - arrived[n * S1 : (n + 1) * S1].astype(F32)
            for k, at in last_jobs[n]:
                acc = acc - dot_t(couple[BOXES[n][0], BOXES[n][1], k], zs[at][...])
            parts.append(acc)
        x = jnp.concatenate(parts, axis=0)
        high = x.astype(BF16)
        low = (x - high.astype(F32)).astype(BF16)
        parent = dot(pick[...], high) + dot(pick[...], low)
        skel_out[...] = parent[:S2]
        red_out[...] = parent[S2:]

        @pl.when(me[0] == 0)
        def _():
            z_out[...] = solve_parent(interp, piv, parent[:S2], parent[S2:])

    skel, red, z0 = call(
        join_body,
        [colour, pick, interp2, pivinv2, couple1, *[have[key] for key in last], from_above, skels],
        [PAR_S, PAR_R, PAR_Z],
        specs=[SMEM],
    )

    (below_pack, above_pack), z0 = after([below_pack, above_pack], z0)
    above_mats, below_mats = shift(below_pack, (1, 0)), shift(above_pack, (-1, 0))

    def sides(z, c):
        return shift(z, (0, 1), (c,)), shift(z, (0, -1), (c,))

    def ends(sums, row):
        colours = (2 * row, 2 * row + 1)
        return shift(sums[0], (-1, 0), colours), shift(sums[1], (1, 0), colours)

    def parent_body(c, me, interp, piv, couple, skel, red, *rest):
        *got, z_out, skel_out = rest

        @pl.when(me[0] != c)
        def _():
            skel_out[...] = skel[...]

        @pl.when(me[0] == c)
        def _():
            acc = skel[...]
            if c % 2:
                acc = acc - (dot(couple[0, 0, 3], got[0][...]) + dot(couple[0, 0, 4], got[1][...]))
            if c >= 2:
                acc = acc - (got[-2][...].astype(F32) + got[-1][...].astype(F32))
            skel_out[...] = acc
            z_out[...] = solve_parent(interp, piv, acc, red[...])

    def parent(c, skel, got):
        return call(
            functools.partial(parent_body, c),
            [colour, interp2, pivinv2, couple2, skel, red, *got],
            [PAR_Z, PAR_S],
            specs=[SMEM],
        )

    def row_body(row, me, above, below, el, er, ol, orr, ze, zo, up_out, down_out):
        for c, (a, own, b) in ((2 * row, (ol, ze, orr)), (2 * row + 1, (el, zo, er))):

            @pl.when(me[0] == c)
            def _():
                for w, out in ((above, up_out), (below, down_out)):
                    total = dot(w[0], a[...]) + dot(w[1], own[...]) + dot(w[2], b[...])
                    out[...] = total.astype(BF16)

    def row(n, even, odd, z_even, z_odd):
        return call(
            functools.partial(row_body, n),
            [colour, above_mats, below_mats, *even, *odd, z_even, z_odd],
            [PAR_M, PAR_M],
            specs=[SMEM],
        )

    side0 = sides(z0, 0)
    z1, skel = parent(1, skel, side0)
    side1 = sides(z1, 1)
    end0 = ends(row(0, side0, side1, z0, z1), 0)
    z2, skel = parent(2, skel, end0)
    side2 = sides(z2, 2)
    z3, skel = parent(3, skel, (*side2, *end0))
    side3 = sides(z3, 3)
    end1 = ends(row(1, side2, side3, z2, z3), 1)

    def early_body(me, interp, couple, skel, z0, z1, z2, z3, al, ar, bl, br, skel_out, z_out):
        for c, own in enumerate((z0, z1, z2, z3)):

            @pl.when(me[0] == c)
            def _():
                zc = own[...]
                z_out[...] = zc
                acc = skel[...] - dot_t(interp[0, 0], zc)
                if c % 2 == 0:
                    xl, xr = ((al, ar), (bl, br))[c // 2]
                    acc = acc - (dot(couple[0, 0, 3], xl[...]) + dot(couple[0, 0, 4], xr[...]))
                skel_out[...] = acc

    skel, red2 = call(
        early_body, [colour, interp2, couple2, skel, z0, z1, z2, z3, *side1, *side3], [PAR_S, PAR_Z], specs=[SMEM]
    )

    def late_body(me, skel, a, b, skel_out):
        @pl.when(me[0] < 2)
        def _():
            skel_out[...] = skel[...] - (a[...].astype(F32) + b[...].astype(F32))

        @pl.when(me[0] >= 2)
        def _():
            skel_out[...] = skel[...]

    (skel2,) = call(late_body, [colour, skel, *end1], [PAR_S], specs=[SMEM])
    return (red1, red2[None, None], skel2[None, None])


def solution(mesh):
    in_specs = (
        P("bx", "by", None, None),
        P("bx", "by", None),
        P("bx", "by", None, None),
        P("bx", "by", None, None),
        P("bx", "by", None, None, None),
        P("bx", "by", None),
        P("bx", "by", None, None),
        P("bx", "by", None, None),
        P("bx", "by", None, None, None),
    )
    out_specs = (P("bx", "by", None, None), P("bx", "by", None, None), P("bx", "by", None, None))
    return jax.shard_map(work, mesh=mesh, in_specs=in_specs, out_specs=out_specs, check_vma=False)
```

```python
import functools

import jax
import jax.numpy as jnp
from jax import lax
from jax.experimental import pallas as pl
from jax.experimental.pallas import tpu as pltpu
from jax.sharding import PartitionSpec as P


S1, R1, P1 = 96, 160, 256
S2, R2, P2 = 128, 256, 384
K = 384
OFFSETS = [(-1, -1), (-1, 0), (-1, 1), (0, -1), (0, 1), (1, -1), (1, 0), (1, 1)]
BOXES = [(0, 0), (0, 1), (1, 0), (1, 1)]
F32, BF16 = jnp.float32, jnp.bfloat16
LEAF_S, LEAF_R, LEAF_Z = ((4, S1, K), F32), ((3, R1, K), F32), ((R1, K), BF16)
LEAF_W, LEAF_M = ((5, R1, S1), BF16), ((2 * S1, K), BF16)
PAR_S, PAR_R, PAR_Z, PAR_M = ((S2, K), F32), ((R2, K), F32), ((R2, K), BF16), ((S2, K), BF16)


UP_TERMS = [((1, 0), (6, 7)), ((1, 1), (5, 6, 7))]
DOWN_TERMS = [((0, 0), (1, 2)), ((0, 1), (0, 1, 2))]

PACKS = {
    (1, 1): (6, 2, (0, 1)),
    (1, -1): (5, 1, (1,)),
    (1, 0): (5, 3, (0, 1, 2)),
    (-1, 1): (1, 2, (0, 1)),
    (-1, -1): (0, 1, (1,)),
    (-1, 0): (0, 3, (0, 1, 2)),
}
CORNERS = [(-1, -1), (-1, 1), (1, -1), (1, 1)]
ENDS = [(-1, 0), (1, 0)]


def dot(a, b):
    return lax.dot_general(a, b, (((1,), (0,)), ((), ())), preferred_element_type=F32)


def dot_t(a, b):
    return lax.dot_general(a, b, (((0,), (0,)), ((), ())), preferred_element_type=F32)


def source(box, k):
    row, col = box[0] + OFFSETS[k][0], box[1] + OFFSETS[k][1]
    return (row % 2) * 2 + col % 2, (row // 2, col // 2)


def reordered(x, perm, rows):
    pick = (lax.broadcasted_iota(jnp.int32, (rows, rows), 0) == perm).astype(F32).astype(BF16)
    high = x.astype(BF16)
    low = (x - high.astype(F32)).astype(BF16)
    return dot_t(pick, high) + dot_t(pick, low)


SMEM, VMEM, ANY, HBM = (pl.BlockSpec(memory_space=s) for s in (pltpu.SMEM, pltpu.VMEM, pl.ANY, pltpu.HBM))


def call(body, ins, outs, specs=(), scratch=(), alias=None):
    specs = list(specs) + [VMEM] * (len(ins) - len(specs))
    return pl.pallas_call(
        body,
        out_shape=[jax.ShapeDtypeStruct(s, d) for s, d in outs],
        in_specs=specs,
        out_specs=[VMEM] * len(outs),
        scratch_shapes=list(scratch),
        input_output_aliases=alias or {},
        compiler_params=pltpu.CompilerParams(vmem_limit_bytes=20 * 1024 * 1024),
        cost_estimate=pl.CostEstimate(flops=300_000_000, bytes_accessed=2_000_000, transcendentals=0),
    )(*ins)


def pairs(dx, dy, colours):
    nx, ny = lax.axis_size("bx"), lax.axis_size("by")
    out = []
    for i in range(nx):
        for j in range(ny):
            if (i % 2) * 2 + j % 2 in colours and 0 <= i + dx < nx and 0 <= j + dy < ny:
                out.append((i * ny + j, (i + dx) * ny + j + dy))
    return out


def shift(x, to, colours=(0, 1, 2, 3)):
    return lax.ppermute(x, ("bx", "by"), pairs(*to, colours))


def after(x, value):
    return lax.optimization_barrier((x, value))


def first_body(rhs, perm, interp, piv, z_out, skel_out, x, p, t, v, sems):
    jobs = [(rhs.at[0, 0], x), (perm, p), (interp.at[0, 0], t), (piv.at[0, 0], v)]
    copies = [pltpu.make_async_copy(a, b, sems.at[n]) for n, (a, b) in enumerate(jobs)]
    for c in copies:
        c.start()
    for c in copies:
        c.wait()
    leaf = reordered(x[...], p[0, 0:1, :], P1)
    skel = leaf[:S1]
    diff = leaf[S1:] - dot(t[...], skel.astype(BF16))
    z_out[...] = dot(v[...], diff.astype(BF16)).astype(BF16)
    skel_out[...] = skel


def pack_body(couple, tie, up_out, down_out, sems):
    jobs = []
    for terms, out in ((UP_TERMS, up_out), (DOWN_TERMS, down_out)):
        at = 0
        for (i, j), ks in terms:
            jobs.append((couple.at[i, j, pl.ds(ks[0], len(ks))], out.at[pl.ds(at, len(ks))]))
            at += len(ks)
    copies = [pltpu.make_async_copy(a, b, sems.at[n]) for n, (a, b) in enumerate(jobs)]
    for c in copies:
        c.start()
    for c in copies:
        c.wait()


def spread_body(rhs, perm, interp, couple, z, skel0, skels, reds):
    zc = z[...]
    skels[0] = skel0[...] - dot_t(interp[0, 0], zc)
    for n in (1, 2, 3):
        i, j = BOXES[n]
        leaf = reordered(rhs[i, j], perm[i, j : j + 1, :], P1)
        reds[n - 1] = leaf[S1:]
        acc = leaf[:S1]
        for k in range(8):
            if source((i, j), k) == (0, (0, 0)):
                acc = acc - dot_t(couple[i, j, k], zc)
        skels[n] = acc


def solve_body(colour, ks, part, interp, piv, couple, skels, reds, *rest):
    zs, (*arrived, z_out, out) = rest[: len(ks)], rest[len(ks) :]
    i, j = BOXES[colour]
    acc = skels[colour]
    if part is not None:
        acc = acc - arrived[0][part * S1 : (part + 1) * S1].astype(F32)
    for k, z in zip(ks, zs):
        acc = acc - dot_t(couple[i, j, k], z[...])
    diff = reds[colour - 1] - dot(interp[i, j], acc.astype(BF16))
    z_out[...] = dot(piv[i, j], diff.astype(BF16)).astype(BF16)
    out[...] = skels[...]
    out[colour] = acc


def sum_body(terms, left, own, right, mats, out):
    values, at = (left[...], own[...], right[...]), 0
    for n, (_, ks) in enumerate(terms):
        total = None
        for w in range(len(ks)):
            term = dot_t(mats[at], values[w])
            total = term if total is None else total + term
            at += 1
        out[n * S1 : (n + 1) * S1] = total.astype(BF16)


def update_body(own, jobs, n_z, part, interp, couple, *refs):
    zs, (skels, *arrived, out) = refs[:n_z], refs[n_z:]
    for n in range(4):
        i, j = BOXES[n]
        acc = skels[n]
        if n == own:
            acc = acc - dot_t(interp[i, j], zs[0][...])
        if part == n:
            acc = acc - arrived[0][S1 : 2 * S1].astype(F32)
        for k, at in jobs[n]:
            acc = acc - dot_t(couple[i, j, k], zs[at][...])
        out[n] = acc


def pick_body(perm, couple, tie, pick_out, *rest):
    packs, sems = rest[:-1], rest[-1]
    copies = [
        pltpu.make_async_copy(couple.at[0, 0, pl.ds(k, n)], out, sems.at[at])
        for at, ((k, n, _), out) in enumerate(zip(PACKS.values(), packs))
    ]
    for c in copies:
        c.start()
    hit = (lax.broadcasted_iota(jnp.int32, (P2, P2), 0) == perm[0]).astype(F32)
    pick_out[...] = hit.T.astype(BF16)
    for c in copies:
        c.wait()


def jobs_of(order, drop=()):
    jobs = [[], [], [], []]
    for n in range(4):
        for k in range(8):
            where = source(BOXES[n], k)
            if where in order and (n, where) not in drop:
                jobs[n].append((k, order.index(where)))
    return jobs


def work(rhs, perm1, interp1, pivinv1, couple1, perm2, interp2, pivinv2, couple2):
    couple1 = couple1.swapaxes(3, 4)
    have = {}
    here = (0, 0)

    def solve(colour, keys, skels, reds, arrived=None, part=None):
        box = BOXES[colour]
        ks, zs = [], []
        for k in range(8):
            if source(box, k) in keys:
                ks.append(k)
                zs.append(have[source(box, k)])
        ins = [interp1, pivinv1, couple1, skels, reds, *zs] + ([arrived] if arrived is not None else [])
        body = functools.partial(solve_body, colour, ks, part)
        z, skels = call(body, ins, [LEAF_Z, LEAF_S])
        have[(colour, here)] = z
        return z, skels

    def total(terms, left, own, right, mats):
        return call(functools.partial(sum_body, terms), [left, own, right, mats], [LEAF_M])[0]

    def update(own, keys, skels, drop=(), arrived=None, part=None):
        order = [(own, here), *keys]
        ins = [interp1, couple1, *[have[key] for key in order], skels] + ([arrived] if arrived is not None else [])
        body = functools.partial(update_body, own, jobs_of(order, drop), len(order), part)
        return call(body, ins, [LEAF_S])[0]

    z00, skel0 = call(
        first_body,
        [pltpu.with_memory_space_constraint(x, pltpu.HBM) for x in (rhs, perm1, interp1, pivinv1)],
        [LEAF_Z, ((S1, K), F32)],
        specs=[HBM] * 4,
        scratch=[
            pltpu.VMEM((P1, K), F32),
            pltpu.VMEM((2, 2, P1), jnp.int32),
            pltpu.VMEM((R1, S1), BF16),
            pltpu.VMEM((R1, R1), BF16),
            pltpu.SemaphoreType.DMA((4,)),
        ],
    )
    have[(0, here)] = z00
    z00r = have[(0, (0, 1))] = shift(z00, (0, -1))
    up_pack, down_pack = call(
        pack_body,
        [pltpu.with_memory_space_constraint(couple1, pltpu.HBM), z00],
        [LEAF_W, LEAF_W],
        specs=[HBM, ANY],
        scratch=[pltpu.SemaphoreType.DMA((4,))],
    )
    up_mats = shift(up_pack, (1, 0))
    down_mats = shift(down_pack, (-1, 0))
    skels, reds = call(spread_body, [rhs, perm1, interp1, couple1, z00, skel0], [LEAF_S, LEAF_R])
    z01, skels = solve(1, {(0, (0, 1))}, skels, reds)
    have[(1, (1, -1))] = shift(z01, (-1, 1))
    from_below = shift(total(UP_TERMS, z00, z01, z00r, up_mats), (-1, 0))
    have[(1, (0, -1))] = shift(z01, (0, 1))
    skels = update(1, [(0, (0, 1))], skels, drop=[(1, (0, (0, 1)))])
    z10, skels = solve(2, {(1, (0, -1)), (1, (1, -1))}, skels, reds, arrived=from_below, part=0)
    z10r = have[(2, (0, 1))] = shift(z10, (0, -1))
    skels = update(2, [(1, (0, -1))], skels, drop=[(2, (1, (0, -1)))], arrived=from_below, part=3)
    z11, skels = solve(3, {(2, (0, 1))}, skels, reds)
    have[(3, (-1, -1))] = shift(z11, (1, 1))
    from_above = shift(total(DOWN_TERMS, z10, z11, z10r, down_mats), (1, 0))
    have[(3, (0, -1))] = shift(z11, (0, 1))
    skels = update(3, [(2, (0, 1))], skels, drop=[(3, (2, (0, 1)))])
    pick, *packs = call(
        pick_body,
        [perm2, pltpu.with_memory_space_constraint(couple2, pltpu.HBM), z11],
        [((P2, P2), BF16)] + [((n, S2, R2), BF16) for _, n, _ in PACKS.values()],
        specs=[VMEM, HBM, ANY],
        scratch=[pltpu.SemaphoreType.DMA((6,))],
    )
    red1 = jnp.stack([z00, z01, z10, z11]).reshape(2, 2, R1, K)

    colour = ((lax.axis_index("bx") % 2) * 2 + lax.axis_index("by") % 2).astype(jnp.int32).reshape(1)
    last = [(3, (0, -1)), (3, (-1, -1))]
    last_jobs = jobs_of(last)

    def solve_parent(interp, piv, skel, red):
        diff = red - dot(interp[0, 0], skel.astype(BF16))
        return dot(piv[0, 0], diff.astype(BF16)).astype(BF16)

    def join_body(me, pick, interp, piv, couple, za, zb, arrived, children, skel_out, red_out, z_out):
        zs = [za, zb]
        parts = []
        for n in range(4):
            acc = children[n]
            if n < 2:
                acc = acc - arrived[n * S1 : (n + 1) * S1].astype(F32)
            for k, at in last_jobs[n]:
                acc = acc - dot_t(couple[BOXES[n][0], BOXES[n][1], k], zs[at][...])
            parts.append(acc)
        x = jnp.concatenate(parts, axis=0)
        high = x.astype(BF16)
        low = (x - high.astype(F32)).astype(BF16)
        parent = dot(pick[...], high) + dot(pick[...], low)
        skel_out[...] = parent[:S2]
        red_out[...] = parent[S2:]

        @pl.when(me[0] == 0)
        def _():
            z_out[...] = solve_parent(interp, piv, parent[:S2], parent[S2:])

    skel, red, z0 = call(
        join_body,
        [colour, pick, interp2, pivinv2, couple1, *[have[key] for key in last], from_above, skels],
        [PAR_S, PAR_R, PAR_Z],
        specs=[SMEM],
    )

    def sides(z, c):
        return shift(z, (0, 1), (c,)), shift(z, (0, -1), (c,))

    def odd_body(c, me, interp, piv, couple, skel, red, zl, zr, *rest):
        if c == 3:
            arrived, rest = rest[:2], rest[2:]
        ws, (z_out, skel_out), sums = rest[:6], rest[6:8], rest[8:]

        @pl.when(me[0] != c)
        def _():
            skel_out[...] = skel[...]

        @pl.when(me[0] == c)
        def _():
            acc = skel[...]
            if c == 3:
                acc = acc - arrived[0][...].astype(F32) - arrived[1][...].astype(F32)
            acc = acc - (dot(couple[0, 0, 3], zl[...]) + dot(couple[0, 0, 4], zr[...]))
            skel_out[...] = acc
            z = solve_parent(interp, piv, acc, red[...])
            z_out[...] = z
            values = (zl[...], z, zr[...])
            for (_, _, which), w, out in zip(PACKS.values(), ws, sums):
                total = None
                for n, v in enumerate(which):
                    term = dot(w[n], values[v])
                    total = term if total is None else total + term
                out[...] = total.astype(BF16)

    def odd(c, skel, zl, zr, arrived=()):
        ws = [mats[(-dx, -dy)] for dx, dy in PACKS]
        z, skel, *sums = call(
            functools.partial(odd_body, c),
            [colour, interp2, pivinv2, couple2, skel, red, zl, zr, *arrived, *ws],
            [PAR_Z, PAR_S] + [PAR_M] * 6,
            specs=[SMEM],
        )
        got = {}
        for way in CORNERS + ENDS:
            got[way] = shift(sums[list(PACKS).index((-way[0], -way[1]))], way, (c,))
        return z, skel, got

    def even_body(me, interp, piv, skel, red, a, b, c, d, z_out, skel_out):
        @pl.when(me[0] != 2)
        def _():
            skel_out[...] = skel[...]

        @pl.when(me[0] == 2)
        def _():
            acc = skel[...] - (a[...].astype(F32) + b[...].astype(F32) + c[...].astype(F32) + d[...].astype(F32))
            skel_out[...] = acc
            z_out[...] = solve_parent(interp, piv, acc, red[...])

    zl, zr = sides(z0, 0)
    packs, z0 = after(packs, z0)
    mats = {(-to[0], -to[1]): shift(pack, to, (1, 3) if to[1] == 0 else (0, 2)) for to, pack in zip(PACKS, packs)}
    z1, skel, got1 = odd(1, skel, zl, zr)
    side1 = sides(z1, 1)
    z2, skel = call(
        even_body, [colour, interp2, pivinv2, skel, red, *[got1[way] for way in CORNERS]], [PAR_Z, PAR_S], specs=[SMEM]
    )
    zl, zr = sides(z2, 2)
    z3, skel, got3 = odd(3, skel, zl, zr, [got1[way] for way in ENDS])
    side3 = sides(z3, 3)

    def early_body(me, interp, couple, skel, z0, z1, z2, z3, xl, xr, skel_out, z_out):
        for c, own in enumerate((z0, z1, z2, z3)):

            @pl.when(me[0] == c)
            def _():
                zc = own[...]
                z_out[...] = zc
                acc = skel[...] - dot_t(interp[0, 0], zc)
                if c == 0:
                    acc = acc - (dot(couple[0, 0, 3], xl[...]) + dot(couple[0, 0, 4], xr[...]))
                skel_out[...] = acc

    skel, red2 = call(
        early_body, [colour, interp2, couple2, skel, z0, z1, z2, z3, *side1], [PAR_S, PAR_Z], specs=[SMEM]
    )

    def late_body(me, couple, skel, a, b, c, d, e, f, xl, xr, skel_out):
        @pl.when(me[0] == 0)
        def _():
            skel_out[...] = skel[...] - (
                a[...].astype(F32) + b[...].astype(F32) + c[...].astype(F32) + d[...].astype(F32)
            )

        @pl.when(me[0] == 1)
        def _():
            skel_out[...] = skel[...] - (e[...].astype(F32) + f[...].astype(F32))

        @pl.when(me[0] == 2)
        def _():
            skel_out[...] = skel[...] - (dot(couple[0, 0, 3], xl[...]) + dot(couple[0, 0, 4], xr[...]))

        @pl.when(me[0] == 3)
        def _():
            skel_out[...] = skel[...]

    (skel2,) = call(
        late_body, [colour, couple2, skel, *[got3[way] for way in CORNERS + ENDS], *side3], [PAR_S], specs=[SMEM]
    )
    return (red1, red2[None, None], skel2[None, None])


def solution(mesh):
    in_specs = (
        P("bx", "by", None, None),
        P("bx", "by", None),
        P("bx", "by", None, None),
        P("bx", "by", None, None),
        P("bx", "by", None, None, None),
        P("bx", "by", None),
        P("bx", "by", None, None),
        P("bx", "by", None, None),
        P("bx", "by", None, None, None),
    )
    out_specs = (P("bx", "by", None, None), P("bx", "by", None, None), P("bx", "by", None, None))
    return jax.shard_map(work, mesh=mesh, in_specs=in_specs, out_specs=out_specs, check_vma=False)
```

```python
import functools

import jax
import jax.numpy as jnp
from jax import lax
from jax.experimental import pallas as pl
from jax.experimental.pallas import tpu as pltpu
from jax.sharding import PartitionSpec as P


S1, R1, P1 = 96, 160, 256
S2, R2, P2 = 128, 256, 384
K = 384
OFFSETS = [(-1, -1), (-1, 0), (-1, 1), (0, -1), (0, 1), (1, -1), (1, 0), (1, 1)]
BOXES = [(0, 0), (0, 1), (1, 0), (1, 1)]
F32, BF16 = jnp.float32, jnp.bfloat16
LEAF_S, LEAF_R, LEAF_Z = ((4, S1, K), F32), ((3, R1, K), F32), ((R1, K), BF16)
PAR_W = ((3, S2, R2), BF16)
LEAF_W, LEAF_M = ((5, R1, S1), BF16), ((2 * S1, K), BF16)
PAR_S, PAR_R, PAR_Z, PAR_M = ((S2, K), F32), ((R2, K), F32), ((R2, K), BF16), ((S2, K), BF16)


UP_TERMS = [((1, 0), (6, 7)), ((1, 1), (5, 6, 7))]
DOWN_TERMS = [((0, 0), (1, 2)), ((0, 1), (0, 1, 2))]

CORNERS = [0, 2, 5, 7]
ENDS = [1, 6]


def dot(a, b):
    return lax.dot_general(a, b, (((1,), (0,)), ((), ())), preferred_element_type=F32)


def dot_t(a, b):
    return lax.dot_general(a, b, (((0,), (0,)), ((), ())), preferred_element_type=F32)


def source(box, k):
    row, col = box[0] + OFFSETS[k][0], box[1] + OFFSETS[k][1]
    return (row % 2) * 2 + col % 2, (row // 2, col // 2)


def reordered(x, perm, rows):
    pick = (lax.broadcasted_iota(jnp.int32, (rows, rows), 0) == perm).astype(F32).astype(BF16)
    high = x.astype(BF16)
    low = (x - high.astype(F32)).astype(BF16)
    return dot_t(pick, high) + dot_t(pick, low)


SMEM, VMEM, ANY, HBM = (pl.BlockSpec(memory_space=s) for s in (pltpu.SMEM, pltpu.VMEM, pl.ANY, pltpu.HBM))


def call(body, ins, outs, specs=(), scratch=(), alias=None):
    specs = list(specs) + [VMEM] * (len(ins) - len(specs))
    return pl.pallas_call(
        body,
        out_shape=[jax.ShapeDtypeStruct(s, d) for s, d in outs],
        in_specs=specs,
        out_specs=[VMEM] * len(outs),
        scratch_shapes=list(scratch),
        input_output_aliases=alias or {},
        compiler_params=pltpu.CompilerParams(vmem_limit_bytes=20 * 1024 * 1024),
        cost_estimate=pl.CostEstimate(flops=300_000_000, bytes_accessed=2_000_000, transcendentals=0),
    )(*ins)


def pairs(dx, dy, colours):
    nx, ny = lax.axis_size("bx"), lax.axis_size("by")
    out = []
    for i in range(nx):
        for j in range(ny):
            if (i % 2) * 2 + j % 2 in colours and 0 <= i + dx < nx and 0 <= j + dy < ny:
                out.append((i * ny + j, (i + dx) * ny + j + dy))
    return out


def shift(x, to, colours=(0, 1, 2, 3)):
    return lax.ppermute(x, ("bx", "by"), pairs(*to, colours))


def after(x, value):
    return lax.optimization_barrier((x, value))


def first_body(rhs, perm, interp, piv, z_out, skel_out, x, p, t, v, sems):
    jobs = [(rhs.at[0, 0], x), (perm, p), (interp.at[0, 0], t), (piv.at[0, 0], v)]
    copies = [pltpu.make_async_copy(a, b, sems.at[n]) for n, (a, b) in enumerate(jobs)]
    for c in copies:
        c.start()
    for c in copies:
        c.wait()
    leaf = reordered(x[...], p[0, 0:1, :], P1)
    skel = leaf[:S1]
    diff = leaf[S1:] - dot(t[...], skel.astype(BF16))
    z_out[...] = dot(v[...], diff.astype(BF16)).astype(BF16)
    skel_out[...] = skel


def pack_body(couple, tie, up_out, down_out, sems):
    jobs = []
    for terms, out in ((UP_TERMS, up_out), (DOWN_TERMS, down_out)):
        at = 0
        for (i, j), ks in terms:
            jobs.append((couple.at[i, j, pl.ds(ks[0], len(ks))], out.at[pl.ds(at, len(ks))]))
            at += len(ks)
    copies = [pltpu.make_async_copy(a, b, sems.at[n]) for n, (a, b) in enumerate(jobs)]
    for c in copies:
        c.start()
    for c in copies:
        c.wait()


def spread_body(rhs, perm, interp, couple, z, skel0, skels, reds):
    zc = z[...]
    skels[0] = skel0[...] - dot_t(interp[0, 0], zc)
    for n in (1, 2, 3):
        i, j = BOXES[n]
        leaf = reordered(rhs[i, j], perm[i, j : j + 1, :], P1)
        reds[n - 1] = leaf[S1:]
        acc = leaf[:S1]
        for k in range(8):
            if source((i, j), k) == (0, (0, 0)):
                acc = acc - dot_t(couple[i, j, k], zc)
        skels[n] = acc


def solve_body(colour, ks, part, interp, piv, couple, skels, reds, *rest):
    zs, (*arrived, z_out, out) = rest[: len(ks)], rest[len(ks) :]
    i, j = BOXES[colour]
    acc = skels[colour]
    if part is not None:
        acc = acc - arrived[0][part * S1 : (part + 1) * S1].astype(F32)
    for k, z in zip(ks, zs):
        acc = acc - dot_t(couple[i, j, k], z[...])
    diff = reds[colour - 1] - dot(interp[i, j], acc.astype(BF16))
    z_out[...] = dot(piv[i, j], diff.astype(BF16)).astype(BF16)
    out[...] = skels[...]
    out[colour] = acc


def sum_body(terms, left, own, right, mats, out):
    values, at = (left[...], own[...], right[...]), 0
    for n, (_, ks) in enumerate(terms):
        total = None
        for w in range(len(ks)):
            term = dot_t(mats[at], values[w])
            total = term if total is None else total + term
            at += 1
        out[n * S1 : (n + 1) * S1] = total.astype(BF16)


def update_body(own, jobs, n_z, part, interp, couple, *refs):
    zs, (skels, *arrived, out) = refs[:n_z], refs[n_z:]
    for n in range(4):
        i, j = BOXES[n]
        acc = skels[n]
        if n == own:
            acc = acc - dot_t(interp[i, j], zs[0][...])
        if part == n:
            acc = acc - arrived[0][S1 : 2 * S1].astype(F32)
        for k, at in jobs[n]:
            acc = acc - dot_t(couple[i, j, k], zs[at][...])
        out[n] = acc


def pick_body(perm, couple, tie, pick_out, below_out, above_out, sems):
    copies = [
        pltpu.make_async_copy(couple.at[0, 0, pl.ds(k, 3)], out, sems.at[at])
        for at, (k, out) in enumerate(((5, below_out), (0, above_out)))
    ]
    for c in copies:
        c.start()
    hit = (lax.broadcasted_iota(jnp.int32, (P2, P2), 0) == perm[0]).astype(F32)
    pick_out[...] = hit.T.astype(BF16)
    for c in copies:
        c.wait()


def jobs_of(order, drop=()):
    jobs = [[], [], [], []]
    for n in range(4):
        for k in range(8):
            where = source(BOXES[n], k)
            if where in order and (n, where) not in drop:
                jobs[n].append((k, order.index(where)))
    return jobs


def work(rhs, perm1, interp1, pivinv1, couple1, perm2, interp2, pivinv2, couple2):
    couple1 = couple1.swapaxes(3, 4)
    have = {}
    here = (0, 0)

    def solve(colour, keys, skels, reds, arrived=None, part=None):
        box = BOXES[colour]
        ks, zs = [], []
        for k in range(8):
            if source(box, k) in keys:
                ks.append(k)
                zs.append(have[source(box, k)])
        ins = [interp1, pivinv1, couple1, skels, reds, *zs] + ([arrived] if arrived is not None else [])
        body = functools.partial(solve_body, colour, ks, part)
        z, skels = call(body, ins, [LEAF_Z, LEAF_S])
        have[(colour, here)] = z
        return z, skels

    def total(terms, left, own, right, mats):
        return call(functools.partial(sum_body, terms), [left, own, right, mats], [LEAF_M])[0]

    def update(own, keys, skels, drop=(), arrived=None, part=None):
        order = [(own, here), *keys]
        ins = [interp1, couple1, *[have[key] for key in order], skels] + ([arrived] if arrived is not None else [])
        body = functools.partial(update_body, own, jobs_of(order, drop), len(order), part)
        return call(body, ins, [LEAF_S])[0]

    z00, skel0 = call(
        first_body,
        [pltpu.with_memory_space_constraint(x, pltpu.HBM) for x in (rhs, perm1, interp1, pivinv1)],
        [LEAF_Z, ((S1, K), F32)],
        specs=[HBM] * 4,
        scratch=[
            pltpu.VMEM((P1, K), F32),
            pltpu.VMEM((2, 2, P1), jnp.int32),
            pltpu.VMEM((R1, S1), BF16),
            pltpu.VMEM((R1, R1), BF16),
            pltpu.SemaphoreType.DMA((4,)),
        ],
    )
    have[(0, here)] = z00
    z00r = have[(0, (0, 1))] = shift(z00, (0, -1))
    up_pack, down_pack = call(
        pack_body,
        [pltpu.with_memory_space_constraint(couple1, pltpu.HBM), z00],
        [LEAF_W, LEAF_W],
        specs=[HBM, ANY],
        scratch=[pltpu.SemaphoreType.DMA((4,))],
    )
    up_mats = shift(up_pack, (1, 0))
    down_mats = shift(down_pack, (-1, 0))
    skels, reds = call(spread_body, [rhs, perm1, interp1, couple1, z00, skel0], [LEAF_S, LEAF_R])
    z01, skels = solve(1, {(0, (0, 1))}, skels, reds)
    have[(1, (1, -1))] = shift(z01, (-1, 1))
    from_below = shift(total(UP_TERMS, z00, z01, z00r, up_mats), (-1, 0))
    have[(1, (0, -1))] = shift(z01, (0, 1))
    skels = update(1, [(0, (0, 1))], skels, drop=[(1, (0, (0, 1)))])
    z10, skels = solve(2, {(1, (0, -1)), (1, (1, -1))}, skels, reds, arrived=from_below, part=0)
    z10r = have[(2, (0, 1))] = shift(z10, (0, -1))
    skels = update(2, [(1, (0, -1))], skels, drop=[(2, (1, (0, -1)))], arrived=from_below, part=3)
    z11, skels = solve(3, {(2, (0, 1))}, skels, reds)
    have[(3, (-1, -1))] = shift(z11, (1, 1))
    from_above = shift(total(DOWN_TERMS, z10, z11, z10r, down_mats), (1, 0))
    have[(3, (0, -1))] = shift(z11, (0, 1))
    skels = update(3, [(2, (0, 1))], skels, drop=[(3, (2, (0, 1)))])
    pick, below_pack, above_pack = call(
        pick_body,
        [perm2, pltpu.with_memory_space_constraint(couple2, pltpu.HBM), z11],
        [((P2, P2), BF16), PAR_W, PAR_W],
        specs=[VMEM, HBM, ANY],
        scratch=[pltpu.SemaphoreType.DMA((2,))],
    )
    red1 = jnp.stack([z00, z01, z10, z11]).reshape(2, 2, R1, K)

    colour = ((lax.axis_index("bx") % 2) * 2 + lax.axis_index("by") % 2).astype(jnp.int32).reshape(1)
    last = [(3, (0, -1)), (3, (-1, -1))]
    last_jobs = jobs_of(last)

    def solve_parent(interp, piv, skel, red):
        diff = red - dot(interp[0, 0], skel.astype(BF16))
        return dot(piv[0, 0], diff.astype(BF16)).astype(BF16)

    def join_body(me, pick, interp, piv, couple, za, zb, arrived, children, skel_out, red_out, z_out):
        zs = [za, zb]
        parts = []
        for n in range(4):
            acc = children[n]
            if n < 2:
                acc = acc - arrived[n * S1 : (n + 1) * S1].astype(F32)
            for k, at in last_jobs[n]:
                acc = acc - dot_t(couple[BOXES[n][0], BOXES[n][1], k], zs[at][...])
            parts.append(acc)
        x = jnp.concatenate(parts, axis=0)
        high = x.astype(BF16)
        low = (x - high.astype(F32)).astype(BF16)
        parent = dot(pick[...], high) + dot(pick[...], low)
        skel_out[...] = parent[:S2]
        red_out[...] = parent[S2:]

        @pl.when(me[0] == 0)
        def _():
            z_out[...] = solve_parent(interp, piv, parent[:S2], parent[S2:])

    skel, red, z0 = call(
        join_body,
        [colour, pick, interp2, pivinv2, couple1, *[have[key] for key in last], from_above, skels],
        [PAR_S, PAR_R, PAR_Z],
        specs=[SMEM],
    )

    def sides(z, c):
        return shift(z, (0, 1), (c,)), shift(z, (0, -1), (c,))

    def ends(up, down, colours):
        return shift(up, (-1, 0), colours), shift(down, (1, 0), colours)

    def parent_body(c, ks, n_sums, me, interp, piv, couple, skel, red, *rest):
        zs, sums, (z_out, skel_out) = rest[: len(ks)], rest[len(ks) : len(ks) + n_sums], rest[len(ks) + n_sums :]

        @pl.when(me[0] != c)
        def _():
            skel_out[...] = skel[...]

        @pl.when(me[0] == c)
        def _():
            acc = skel[...]
            for x in sums:
                acc = acc - x[...].astype(F32)
            for k, z in zip(ks, zs):
                acc = acc - dot(couple[0, 0, k], z[...])
            skel_out[...] = acc
            z_out[...] = solve_parent(interp, piv, acc, red[...])

    def parent(c, skel, ks, zs, sums=()):
        return call(
            functools.partial(parent_body, c, ks, len(sums)),
            [colour, interp2, pivinv2, couple2, skel, red, *zs, *sums],
            [PAR_Z, PAR_S],
            specs=[SMEM],
        )

    def row_body(colours, me, above, below, *rest):
        values, (up_out, down_out) = rest[:-2], rest[-2:]
        for n, c in enumerate(colours):

            @pl.when(me[0] == c)
            def _():
                a, own, b = (v[...] for v in values[3 * n : 3 * n + 3])
                for w, out in ((above, up_out), (below, down_out)):
                    out[...] = (dot(w[0], a) + dot(w[1], own) + dot(w[2], b)).astype(BF16)

    def row(colours, values):
        return call(
            functools.partial(row_body, colours),
            [colour, above_mats, below_mats, *values],
            [PAR_M, PAR_M],
            specs=[SMEM],
        )

    side0 = sides(z0, 0)
    (below_pack, above_pack), z0 = after([below_pack, above_pack], z0)
    above_mats = shift(below_pack, (1, 0), (0, 1, 3))
    below_mats = shift(above_pack, (-1, 0), (0, 1, 3))
    from_below, from_above = ends(z0, z0, (0,))
    z1, skel = parent(1, skel, [3, 4], side0)
    corners = [shift(z1, (-OFFSETS[k][0], -OFFSETS[k][1]), (1,)) for k in CORNERS]
    sums1 = ends(*row((1,), (side0[0], z1, side0[1])), (1,))
    side1 = sides(z1, 1)
    z2, skel = parent(2, skel, [*ENDS, *CORNERS], [from_above, from_below, *corners])
    side2 = sides(z2, 2)
    z3, skel = parent(3, skel, [3, 4], side2, sums1)
    side3 = sides(z3, 3)
    values = (side3[0], z2, side3[1], side2[0], z3, side2[1])
    end1 = ends(*row((2, 3), values), (2, 3))

    def early_body(me, interp, couple, skel, z0, z1, z2, z3, al, ar, bl, br, skel_out, z_out):
        for c, own in enumerate((z0, z1, z2, z3)):

            @pl.when(me[0] == c)
            def _():
                zc = own[...]
                z_out[...] = zc
                acc = skel[...] - dot_t(interp[0, 0], zc)
                if c % 2 == 0:
                    xl, xr = ((al, ar), (bl, br))[c // 2]
                    acc = acc - (dot(couple[0, 0, 3], xl[...]) + dot(couple[0, 0, 4], xr[...]))
                skel_out[...] = acc

    skel, red2 = call(
        early_body, [colour, interp2, couple2, skel, z0, z1, z2, z3, *side1, *side3], [PAR_S, PAR_Z], specs=[SMEM]
    )

    def late_body(me, skel, a, b, skel_out):
        @pl.when(me[0] < 2)
        def _():
            skel_out[...] = skel[...] - (a[...].astype(F32) + b[...].astype(F32))

        @pl.when(me[0] >= 2)
        def _():
            skel_out[...] = skel[...]

    (skel2,) = call(late_body, [colour, skel, *end1], [PAR_S], specs=[SMEM])
    return (red1, red2[None, None], skel2[None, None])


def solution(mesh):
    in_specs = (
        P("bx", "by", None, None),
        P("bx", "by", None),
        P("bx", "by", None, None),
        P("bx", "by", None, None),
        P("bx", "by", None, None, None),
        P("bx", "by", None),
        P("bx", "by", None, None),
        P("bx", "by", None, None),
        P("bx", "by", None, None, None),
    )
    out_specs = (P("bx", "by", None, None), P("bx", "by", None, None), P("bx", "by", None, None))
    return jax.shard_map(work, mesh=mesh, in_specs=in_specs, out_specs=out_specs, check_vma=False)
```

```python
import functools

import jax
import jax.numpy as jnp
from jax import lax
from jax.experimental import pallas as pl
from jax.experimental.pallas import tpu as pltpu
from jax.sharding import PartitionSpec as P


S1, R1, P1 = 96, 160, 256
S2, R2, P2 = 128, 256, 384
K = 384
OFFSETS = [(-1, -1), (-1, 0), (-1, 1), (0, -1), (0, 1), (1, -1), (1, 0), (1, 1)]
BOXES = [(0, 0), (0, 1), (1, 0), (1, 1)]
F32, BF16 = jnp.float32, jnp.bfloat16
LEAF_S, LEAF_R, LEAF_Z = ((4, S1, K), F32), ((3, R1, K), F32), ((R1, K), BF16)
PAR_W = ((3, S2, R2), BF16)
LEAF_W, LEAF_M = ((5, R1, S1), BF16), ((2 * S1, K), BF16)
PAR_S, PAR_R, PAR_Z, PAR_M = ((S2, K), F32), ((R2, K), F32), ((R2, K), BF16), ((S2, K), BF16)


UP_TERMS = [((1, 0), (6, 7)), ((1, 1), (5, 6, 7))]
DOWN_TERMS = [((0, 0), (1, 2)), ((0, 1), (0, 1, 2))]

CORNERS = [0, 2, 5, 7]
ENDS = [1, 6]


def dot(a, b):
    return lax.dot_general(a, b, (((1,), (0,)), ((), ())), preferred_element_type=F32)


def dot_t(a, b):
    return lax.dot_general(a, b, (((0,), (0,)), ((), ())), preferred_element_type=F32)


def source(box, k):
    row, col = box[0] + OFFSETS[k][0], box[1] + OFFSETS[k][1]
    return (row % 2) * 2 + col % 2, (row // 2, col // 2)


def reordered(x, perm, rows):
    pick = (lax.broadcasted_iota(jnp.int32, (rows, rows), 0) == perm).astype(F32).astype(BF16)
    high = x.astype(BF16)
    low = (x - high.astype(F32)).astype(BF16)
    return dot_t(pick, high) + dot_t(pick, low)


SMEM, VMEM, ANY, HBM = (pl.BlockSpec(memory_space=s) for s in (pltpu.SMEM, pltpu.VMEM, pl.ANY, pltpu.HBM))


def call(body, ins, outs, specs=(), scratch=(), alias=None):
    specs = list(specs) + [VMEM] * (len(ins) - len(specs))
    return pl.pallas_call(
        body,
        out_shape=[jax.ShapeDtypeStruct(s, d) for s, d in outs],
        in_specs=specs,
        out_specs=[VMEM] * len(outs),
        scratch_shapes=list(scratch),
        input_output_aliases=alias or {},
        compiler_params=pltpu.CompilerParams(vmem_limit_bytes=20 * 1024 * 1024),
        cost_estimate=pl.CostEstimate(flops=300_000_000, bytes_accessed=2_000_000, transcendentals=0),
    )(*ins)


def pairs(dx, dy, colours):
    nx, ny = lax.axis_size("bx"), lax.axis_size("by")
    out = []
    for i in range(nx):
        for j in range(ny):
            if (i % 2) * 2 + j % 2 in colours and 0 <= i + dx < nx and 0 <= j + dy < ny:
                out.append((i * ny + j, (i + dx) * ny + j + dy))
    return out


def shift(x, to, colours=(0, 1, 2, 3)):
    return lax.ppermute(x, ("bx", "by"), pairs(*to, colours))


def after(x, value):
    return lax.optimization_barrier((x, value))


def first_body(rhs, perm, interp, piv, z_out, skel_out, x, p, t, v, sems):
    jobs = [(rhs.at[0, 0], x), (perm, p), (interp.at[0, 0], t), (piv.at[0, 0], v)]
    copies = [pltpu.make_async_copy(a, b, sems.at[n]) for n, (a, b) in enumerate(jobs)]
    for c in copies:
        c.start()
    for c in copies:
        c.wait()
    leaf = reordered(x[...], p[0, 0:1, :], P1)
    skel = leaf[:S1]
    diff = leaf[S1:] - dot(t[...], skel.astype(BF16))
    z_out[...] = dot(v[...], diff.astype(BF16)).astype(BF16)
    skel_out[...] = skel


def pack_body(couple, tie, up_out, down_out, sems):
    jobs = []
    for terms, out in ((UP_TERMS, up_out), (DOWN_TERMS, down_out)):
        at = 0
        for (i, j), ks in terms:
            jobs.append((couple.at[i, j, pl.ds(ks[0], len(ks))], out.at[pl.ds(at, len(ks))]))
            at += len(ks)
    copies = [pltpu.make_async_copy(a, b, sems.at[n]) for n, (a, b) in enumerate(jobs)]
    for c in copies:
        c.start()
    for c in copies:
        c.wait()


def spread_body(rhs, perm, interp, couple, z, skel0, skels, reds):
    zc = z[...]
    skels[0] = skel0[...] - dot_t(interp[0, 0], zc)
    for n in (1, 2, 3):
        i, j = BOXES[n]
        leaf = reordered(rhs[i, j], perm[i, j : j + 1, :], P1)
        reds[n - 1] = leaf[S1:]
        acc = leaf[:S1]
        for k in range(8):
            if source((i, j), k) == (0, (0, 0)):
                acc = acc - dot_t(couple[i, j, k], zc)
        skels[n] = acc


def solve_body(colour, ks, part, interp, piv, couple, skels, reds, *rest):
    zs, (*arrived, z_out, out) = rest[: len(ks)], rest[len(ks) :]
    i, j = BOXES[colour]
    acc = skels[colour]
    if part is not None:
        acc = acc - arrived[0][part * S1 : (part + 1) * S1].astype(F32)
    for k, z in zip(ks, zs):
        acc = acc - dot_t(couple[i, j, k], z[...])
    diff = reds[colour - 1] - dot(interp[i, j], acc.astype(BF16))
    z_out[...] = dot(piv[i, j], diff.astype(BF16)).astype(BF16)
    out[...] = skels[...]
    out[colour] = acc


def sum_body(terms, left, own, right, mats, out):
    values, at = (left[...], own[...], right[...]), 0
    for n, (_, ks) in enumerate(terms):
        total = None
        for w in range(len(ks)):
            term = dot_t(mats[at], values[w])
            total = term if total is None else total + term
            at += 1
        out[n * S1 : (n + 1) * S1] = total.astype(BF16)


def update_body(own, jobs, n_z, part, interp, couple, *refs):
    zs, (skels, *arrived, out) = refs[:n_z], refs[n_z:]
    for n in range(4):
        i, j = BOXES[n]
        acc = skels[n]
        if n == own:
            acc = acc - dot_t(interp[i, j], zs[0][...])
        if part == n:
            acc = acc - arrived[0][S1 : 2 * S1].astype(F32)
        for k, at in jobs[n]:
            acc = acc - dot_t(couple[i, j, k], zs[at][...])
        out[n] = acc


def pick_body(perm, couple, tie, pick_out, below_out, above_out, sems):
    copies = [
        pltpu.make_async_copy(couple.at[0, 0, pl.ds(k, 3)], out, sems.at[at])
        for at, (k, out) in enumerate(((5, below_out), (0, above_out)))
    ]
    for c in copies:
        c.start()
    hit = (lax.broadcasted_iota(jnp.int32, (P2, P2), 0) == perm[0]).astype(F32)
    pick_out[...] = hit.T.astype(BF16)
    for c in copies:
        c.wait()


def jobs_of(order, drop=()):
    jobs = [[], [], [], []]
    for n in range(4):
        for k in range(8):
            where = source(BOXES[n], k)
            if where in order and (n, where) not in drop:
                jobs[n].append((k, order.index(where)))
    return jobs


def work(rhs, perm1, interp1, pivinv1, couple1, perm2, interp2, pivinv2, couple2):
    couple1 = couple1.swapaxes(3, 4)
    have = {}
    here = (0, 0)

    def solve(colour, keys, skels, reds, arrived=None, part=None):
        box = BOXES[colour]
        ks, zs = [], []
        for k in range(8):
            if source(box, k) in keys:
                ks.append(k)
                zs.append(have[source(box, k)])
        ins = [interp1, pivinv1, couple1, skels, reds, *zs] + ([arrived] if arrived is not None else [])
        body = functools.partial(solve_body, colour, ks, part)
        z, skels = call(body, ins, [LEAF_Z, LEAF_S])
        have[(colour, here)] = z
        return z, skels

    def total(terms, left, own, right, mats):
        return call(functools.partial(sum_body, terms), [left, own, right, mats], [LEAF_M])[0]

    def update(own, keys, skels, drop=(), arrived=None, part=None):
        order = [(own, here), *keys]
        ins = [interp1, couple1, *[have[key] for key in order], skels] + ([arrived] if arrived is not None else [])
        body = functools.partial(update_body, own, jobs_of(order, drop), len(order), part)
        return call(body, ins, [LEAF_S])[0]

    z00, skel0 = call(
        first_body,
        [pltpu.with_memory_space_constraint(x, pltpu.HBM) for x in (rhs, perm1, interp1, pivinv1)],
        [LEAF_Z, ((S1, K), F32)],
        specs=[HBM] * 4,
        scratch=[
            pltpu.VMEM((P1, K), F32),
            pltpu.VMEM((2, 2, P1), jnp.int32),
            pltpu.VMEM((R1, S1), BF16),
            pltpu.VMEM((R1, R1), BF16),
            pltpu.SemaphoreType.DMA((4,)),
        ],
    )
    have[(0, here)] = z00
    z00r = have[(0, (0, 1))] = shift(z00, (0, -1))
    up_pack, down_pack = call(
        pack_body,
        [pltpu.with_memory_space_constraint(couple1, pltpu.HBM), z00],
        [LEAF_W, LEAF_W],
        specs=[HBM, ANY],
        scratch=[pltpu.SemaphoreType.DMA((4,))],
    )
    up_mats = shift(up_pack, (1, 0))
    down_mats = shift(down_pack, (-1, 0))
    skels, reds = call(spread_body, [rhs, perm1, interp1, couple1, z00, skel0], [LEAF_S, LEAF_R])
    z01, skels = solve(1, {(0, (0, 1))}, skels, reds)
    have[(1, (1, -1))] = shift(z01, (-1, 1))
    from_below = shift(total(UP_TERMS, z00, z01, z00r, up_mats), (-1, 0))
    have[(1, (0, -1))] = shift(z01, (0, 1))
    skels = update(1, [(0, (0, 1))], skels, drop=[(1, (0, (0, 1)))])
    z10, skels = solve(2, {(1, (0, -1)), (1, (1, -1))}, skels, reds, arrived=from_below, part=0)
    z10r = have[(2, (0, 1))] = shift(z10, (0, -1))
    skels = update(2, [(1, (0, -1))], skels, drop=[(2, (1, (0, -1)))], arrived=from_below, part=3)
    z11, skels = solve(3, {(2, (0, 1))}, skels, reds)
    have[(3, (-1, -1))] = shift(z11, (1, 1))
    from_above = shift(total(DOWN_TERMS, z10, z11, z10r, down_mats), (1, 0))
    have[(3, (0, -1))] = shift(z11, (0, 1))
    skels = update(3, [(2, (0, 1))], skels, drop=[(3, (2, (0, 1)))])
    pick, below_pack, above_pack = call(
        pick_body,
        [perm2, pltpu.with_memory_space_constraint(couple2, pltpu.HBM), z11],
        [((P2, P2), BF16), PAR_W, PAR_W],
        specs=[VMEM, HBM, ANY],
        scratch=[pltpu.SemaphoreType.DMA((2,))],
    )
    red1 = jnp.stack([z00, z01, z10, z11]).reshape(2, 2, R1, K)

    colour = ((lax.axis_index("bx") % 2) * 2 + lax.axis_index("by") % 2).astype(jnp.int32).reshape(1)
    last = [(3, (0, -1)), (3, (-1, -1))]
    last_jobs = jobs_of(last)

    def solve_parent(interp, piv, skel, red):
        diff = red - dot(interp[0, 0], skel.astype(BF16))
        return dot(piv[0, 0], diff.astype(BF16)).astype(BF16)

    def join_body(me, pick, interp, piv, couple, za, zb, arrived, children, skel_out, red_out, z_out):
        zs = [za, zb]
        parts = []
        for n in range(4):
            acc = children[n]
            if n < 2:
                acc = acc - arrived[n * S1 : (n + 1) * S1].astype(F32)
            for k, at in last_jobs[n]:
                acc = acc - dot_t(couple[BOXES[n][0], BOXES[n][1], k], zs[at][...])
            parts.append(acc)
        x = jnp.concatenate(parts, axis=0)
        high = x.astype(BF16)
        low = (x - high.astype(F32)).astype(BF16)
        parent = dot(pick[...], high) + dot(pick[...], low)
        skel_out[...] = parent[:S2]
        red_out[...] = parent[S2:]

        @pl.when(me[0] == 0)
        def _():
            z_out[...] = solve_parent(interp, piv, parent[:S2], parent[S2:])

    skel, red, z0 = call(
        join_body,
        [colour, pick, interp2, pivinv2, couple1, *[have[key] for key in last], from_above, skels],
        [PAR_S, PAR_R, PAR_Z],
        specs=[SMEM],
    )

    def sides(z, colours):
        return shift(z, (0, 1), colours), shift(z, (0, -1), colours)

    def ends(up, down, colours):
        return shift(up, (-1, 0), colours), shift(down, (1, 0), colours)

    def parent_body(c, ks, n_sums, me, interp, piv, couple, skel, red, *rest):
        zs, sums = rest[: len(ks)], rest[len(ks) : len(ks) + n_sums]
        *held, z_out, skel_out = rest[len(ks) + n_sums :]
        if held:

            @pl.when(me[0] == c - 1)
            def _():
                z_out[...] = held[0][...]

        @pl.when(me[0] != c)
        def _():
            skel_out[...] = skel[...]

        @pl.when(me[0] == c)
        def _():
            acc = skel[...]
            for x in sums:
                acc = acc - x[...].astype(F32)
            for k, z in zip(ks, zs):
                acc = acc - dot(couple[0, 0, k], z[...])
            skel_out[...] = acc
            z_out[...] = solve_parent(interp, piv, acc, red[...])

    def parent(c, skel, ks, zs, sums=(), held=()):
        return call(
            functools.partial(parent_body, c, ks, len(sums)),
            [colour, interp2, pivinv2, couple2, skel, red, *zs, *sums, *held],
            [PAR_Z, PAR_S],
            specs=[SMEM],
        )

    def row_body(colours, me, above, below, *rest):
        values, (up_out, down_out) = rest[:-2], rest[-2:]
        for n, c in enumerate(colours):

            @pl.when(me[0] == c)
            def _():
                a, own, b = (v[...] for v in values[3 * n : 3 * n + 3])
                for w, out in ((above, up_out), (below, down_out)):
                    out[...] = (dot(w[0], a) + dot(w[1], own) + dot(w[2], b)).astype(BF16)

    def row(colours, values):
        return call(
            functools.partial(row_body, colours),
            [colour, above_mats, below_mats, *values],
            [PAR_M, PAR_M],
            specs=[SMEM],
        )

    side0 = sides(z0, (0,))
    z1, skel = parent(1, skel, [3, 4], side0)
    corners = [shift(z1, (-OFFSETS[k][0], -OFFSETS[k][1]), (1,)) for k in CORNERS]
    (below_pack, above_pack), z0 = after([below_pack, above_pack], z0)
    above_mats = shift(below_pack, (1, 0), (0, 1, 3))
    below_mats = shift(above_pack, (-1, 0), (0, 1, 3))
    from_below, from_above = ends(z0, z0, (0,))
    z2, skel = parent(2, skel, [*ENDS, *CORNERS], [from_above, from_below, *corners], held=[z1])
    side2 = sides(z2, (1, 2))
    sums1 = ends(*row((1,), (side0[0], z1, side0[1])), (1,))
    z3, skel = parent(3, skel, [3, 4], side2, sums1)
    side3 = sides(z3, (3,))
    values = (side3[0], z2, side3[1], side2[0], z3, side2[1])
    end1 = ends(*row((2, 3), values), (2, 3))

    def early_body(me, interp, couple, skel, z0, z1, z2, z3, al, ar, bl, br, skel_out, z_out):
        for c, own in enumerate((z0, z1, z2, z3)):

            @pl.when(me[0] == c)
            def _():
                zc = own[...]
                z_out[...] = zc
                acc = skel[...] - dot_t(interp[0, 0], zc)
                if c % 2 == 0:
                    xl, xr = ((al, ar), (bl, br))[c // 2]
                    acc = acc - (dot(couple[0, 0, 3], xl[...]) + dot(couple[0, 0, 4], xr[...]))
                skel_out[...] = acc

    skel, red2 = call(
        early_body, [colour, interp2, couple2, skel, z0, z1, z2, z3, *side2, *side3], [PAR_S, PAR_Z], specs=[SMEM]
    )

    def late_body(me, skel, a, b, skel_out):
        @pl.when(me[0] < 2)
        def _():
            skel_out[...] = skel[...] - (a[...].astype(F32) + b[...].astype(F32))

        @pl.when(me[0] >= 2)
        def _():
            skel_out[...] = skel[...]

    (skel2,) = call(late_body, [colour, skel, *end1], [PAR_S], specs=[SMEM])
    return (red1, red2[None, None], skel2[None, None])


def solution(mesh):
    in_specs = (
        P("bx", "by", None, None),
        P("bx", "by", None),
        P("bx", "by", None, None),
        P("bx", "by", None, None),
        P("bx", "by", None, None, None),
        P("bx", "by", None),
        P("bx", "by", None, None),
        P("bx", "by", None, None),
        P("bx", "by", None, None, None),
    )
    out_specs = (P("bx", "by", None, None), P("bx", "by", None, None), P("bx", "by", None, None))
    return jax.shard_map(work, mesh=mesh, in_specs=in_specs, out_specs=out_specs, check_vma=False)
```

```python
import functools

import jax
import jax.numpy as jnp
from jax import lax
from jax.experimental import pallas as pl
from jax.experimental.pallas import tpu as pltpu
from jax.sharding import PartitionSpec as P


S1, R1, P1 = 96, 160, 256
S2, R2, P2 = 128, 256, 384
K = 384
OFFSETS = [(-1, -1), (-1, 0), (-1, 1), (0, -1), (0, 1), (1, -1), (1, 0), (1, 1)]
BOXES = [(0, 0), (0, 1), (1, 0), (1, 1)]
F32, BF16 = jnp.float32, jnp.bfloat16
LEAF_S, LEAF_R, LEAF_Z = ((4, S1, K), F32), ((3, R1, K), F32), ((R1, K), BF16)
PAR_W = ((3, S2, R2), BF16)
LEAF_W, LEAF_M = ((5, R1, S1), BF16), ((2 * S1, K), BF16)
PAR_S, PAR_R, PAR_Z, PAR_M = ((S2, K), F32), ((R2, K), F32), ((R2, K), BF16), ((S2, K), BF16)


UP_TERMS = [((1, 0), (6, 7)), ((1, 1), (5, 6, 7))]
DOWN_TERMS = [((0, 0), (1, 2)), ((0, 1), (0, 1, 2))]

CORNERS = [0, 2, 5, 7]
ENDS = [1, 6]


def dot(a, b):
    return lax.dot_general(a, b, (((1,), (0,)), ((), ())), preferred_element_type=F32)


def dot_t(a, b):
    return lax.dot_general(a, b, (((0,), (0,)), ((), ())), preferred_element_type=F32)


def source(box, k):
    row, col = box[0] + OFFSETS[k][0], box[1] + OFFSETS[k][1]
    return (row % 2) * 2 + col % 2, (row // 2, col // 2)


def reordered(x, perm, rows):
    pick = (lax.broadcasted_iota(jnp.int32, (rows, rows), 0) == perm).astype(F32).astype(BF16)
    high = x.astype(BF16)
    low = (x - high.astype(F32)).astype(BF16)
    return dot_t(pick, high) + dot_t(pick, low)


SMEM, VMEM, ANY, HBM = (pl.BlockSpec(memory_space=s) for s in (pltpu.SMEM, pltpu.VMEM, pl.ANY, pltpu.HBM))


def call(body, ins, outs, specs=(), scratch=(), alias=None):
    specs = list(specs) + [VMEM] * (len(ins) - len(specs))
    return pl.pallas_call(
        body,
        out_shape=[jax.ShapeDtypeStruct(s, d) for s, d in outs],
        in_specs=specs,
        out_specs=[VMEM] * len(outs),
        scratch_shapes=list(scratch),
        input_output_aliases=alias or {},
        compiler_params=pltpu.CompilerParams(vmem_limit_bytes=20 * 1024 * 1024),
        cost_estimate=pl.CostEstimate(flops=300_000_000, bytes_accessed=2_000_000, transcendentals=0),
    )(*ins)


def pairs(dx, dy, colours):
    nx, ny = lax.axis_size("bx"), lax.axis_size("by")
    out = []
    for i in range(nx):
        for j in range(ny):
            if (i % 2) * 2 + j % 2 in colours and 0 <= i + dx < nx and 0 <= j + dy < ny:
                out.append((i * ny + j, (i + dx) * ny + j + dy))
    return out


def shift(x, to, colours=(0, 1, 2, 3)):
    return lax.ppermute(x, ("bx", "by"), pairs(*to, colours))


def after(x, value):
    return lax.optimization_barrier((x, value))


def pack_jobs(terms, couple, out):
    jobs, at = [], 0
    for (i, j), ks in terms:
        jobs.append((couple.at[i, j, pl.ds(ks[0], len(ks))], out.at[pl.ds(at, len(ks))]))
        at += len(ks)
    return jobs


def first_body(rhs, perm, interp, piv, couple, z_out, skel_out, up_out, x, p, t, v, sems):
    jobs = [(rhs.at[0, 0], x), (perm, p), (interp.at[0, 0], t), (piv.at[0, 0], v), *pack_jobs(UP_TERMS, couple, up_out)]
    copies = [pltpu.make_async_copy(a, b, sems.at[n]) for n, (a, b) in enumerate(jobs)]
    for c in copies:
        c.start()
    for c in copies[:4]:
        c.wait()
    leaf = reordered(x[...], p[0, 0:1, :], P1)
    skel = leaf[:S1]
    diff = leaf[S1:] - dot(t[...], skel.astype(BF16))
    z_out[...] = dot(v[...], diff.astype(BF16)).astype(BF16)
    skel_out[...] = skel
    for c in copies[4:]:
        c.wait()


def pack_body(couple, tie, down_out, sems):
    copies = [pltpu.make_async_copy(a, b, sems.at[n]) for n, (a, b) in enumerate(pack_jobs(DOWN_TERMS, couple, down_out))]
    for c in copies:
        c.start()
    for c in copies:
        c.wait()


def spread_body(rhs, perm, interp, couple, z, skel0, skels, reds):
    zc = z[...]
    skels[0] = skel0[...] - dot_t(interp[0, 0], zc)
    for n in (1, 2, 3):
        i, j = BOXES[n]
        leaf = reordered(rhs[i, j], perm[i, j : j + 1, :], P1)
        reds[n - 1] = leaf[S1:]
        acc = leaf[:S1]
        for k in range(8):
            if source((i, j), k) == (0, (0, 0)):
                acc = acc - dot_t(couple[i, j, k], zc)
        skels[n] = acc


def solve_body(colour, ks, part, interp, piv, couple, skels, reds, *rest):
    zs, (*arrived, z_out, out) = rest[: len(ks)], rest[len(ks) :]
    i, j = BOXES[colour]
    acc = skels[colour]
    if part is not None:
        acc = acc - arrived[0][part * S1 : (part + 1) * S1].astype(F32)
    for k, z in zip(ks, zs):
        acc = acc - dot_t(couple[i, j, k], z[...])
    diff = reds[colour - 1] - dot(interp[i, j], acc.astype(BF16))
    z_out[...] = dot(piv[i, j], diff.astype(BF16)).astype(BF16)
    out[...] = skels[...]
    out[colour] = acc


def sum_body(terms, left, own, right, mats, out):
    values, at = (left[...], own[...], right[...]), 0
    for n, (_, ks) in enumerate(terms):
        total = None
        for w in range(len(ks)):
            term = dot_t(mats[at], values[w])
            total = term if total is None else total + term
            at += 1
        out[n * S1 : (n + 1) * S1] = total.astype(BF16)


def update_body(own, jobs, n_z, part, interp, couple, *refs):
    zs, (skels, *arrived, out) = refs[:n_z], refs[n_z:]
    for n in range(4):
        i, j = BOXES[n]
        acc = skels[n]
        if n == own:
            acc = acc - dot_t(interp[i, j], zs[0][...])
        if part == n:
            acc = acc - arrived[0][S1 : 2 * S1].astype(F32)
        for k, at in jobs[n]:
            acc = acc - dot_t(couple[i, j, k], zs[at][...])
        out[n] = acc


def pick_body(perm, couple, tie, pick_out, below_out, above_out, sems):
    copies = [
        pltpu.make_async_copy(couple.at[0, 0, pl.ds(k, 3)], out, sems.at[at])
        for at, (k, out) in enumerate(((5, below_out), (0, above_out)))
    ]
    for c in copies:
        c.start()
    hit = (lax.broadcasted_iota(jnp.int32, (P2, P2), 0) == perm[0]).astype(F32)
    pick_out[...] = hit.T.astype(BF16)
    for c in copies:
        c.wait()


def jobs_of(order, drop=()):
    jobs = [[], [], [], []]
    for n in range(4):
        for k in range(8):
            where = source(BOXES[n], k)
            if where in order and (n, where) not in drop:
                jobs[n].append((k, order.index(where)))
    return jobs


def work(rhs, perm1, interp1, pivinv1, couple1, perm2, interp2, pivinv2, couple2):
    couple1 = couple1.swapaxes(3, 4)
    have = {}
    here = (0, 0)

    def solve(colour, keys, skels, reds, arrived=None, part=None):
        box = BOXES[colour]
        ks, zs = [], []
        for k in range(8):
            if source(box, k) in keys:
                ks.append(k)
                zs.append(have[source(box, k)])
        ins = [interp1, pivinv1, couple1, skels, reds, *zs] + ([arrived] if arrived is not None else [])
        body = functools.partial(solve_body, colour, ks, part)
        z, skels = call(body, ins, [LEAF_Z, LEAF_S])
        have[(colour, here)] = z
        return z, skels

    def total(terms, left, own, right, mats):
        return call(functools.partial(sum_body, terms), [left, own, right, mats], [LEAF_M])[0]

    def update(own, keys, skels, drop=(), arrived=None, part=None):
        order = [(own, here), *keys]
        ins = [interp1, couple1, *[have[key] for key in order], skels] + ([arrived] if arrived is not None else [])
        body = functools.partial(update_body, own, jobs_of(order, drop), len(order), part)
        return call(body, ins, [LEAF_S])[0]

    z00, skel0, up_pack = call(
        first_body,
        [pltpu.with_memory_space_constraint(x, pltpu.HBM) for x in (rhs, perm1, interp1, pivinv1, couple1)],
        [LEAF_Z, ((S1, K), F32), LEAF_W],
        specs=[HBM] * 5,
        scratch=[
            pltpu.VMEM((P1, K), F32),
            pltpu.VMEM((2, 2, P1), jnp.int32),
            pltpu.VMEM((R1, S1), BF16),
            pltpu.VMEM((R1, R1), BF16),
            pltpu.SemaphoreType.DMA((6,)),
        ],
    )
    have[(0, here)] = z00
    z00r = have[(0, (0, 1))] = shift(z00, (0, -1))
    up_mats = shift(up_pack, (1, 0))
    skels, reds = call(spread_body, [rhs, perm1, interp1, couple1, z00, skel0], [LEAF_S, LEAF_R])
    z01, skels = solve(1, {(0, (0, 1))}, skels, reds)
    have[(1, (1, -1))] = shift(z01, (-1, 1))
    from_below = shift(total(UP_TERMS, z00, z01, z00r, up_mats), (-1, 0))
    have[(1, (0, -1))] = shift(z01, (0, 1))
    skels = update(1, [(0, (0, 1))], skels, drop=[(1, (0, (0, 1)))])
    z10, skels = solve(2, {(1, (0, -1)), (1, (1, -1))}, skels, reds, arrived=from_below, part=0)
    z10r = have[(2, (0, 1))] = shift(z10, (0, -1))
    (down_pack,) = call(
        pack_body,
        [pltpu.with_memory_space_constraint(couple1, pltpu.HBM), z01],
        [LEAF_W],
        specs=[HBM, ANY],
        scratch=[pltpu.SemaphoreType.DMA((2,))],
    )
    down_mats = shift(down_pack, (-1, 0))
    skels = update(2, [(1, (0, -1))], skels, drop=[(2, (1, (0, -1)))], arrived=from_below, part=3)
    z11, skels = solve(3, {(2, (0, 1))}, skels, reds)
    have[(3, (-1, -1))] = shift(z11, (1, 1))
    from_above = shift(total(DOWN_TERMS, z10, z11, z10r, down_mats), (1, 0))
    have[(3, (0, -1))] = shift(z11, (0, 1))
    skels = update(3, [(2, (0, 1))], skels, drop=[(3, (2, (0, 1)))])
    pick, below_pack, above_pack = call(
        pick_body,
        [perm2, pltpu.with_memory_space_constraint(couple2, pltpu.HBM), z11],
        [((P2, P2), BF16), PAR_W, PAR_W],
        specs=[VMEM, HBM, ANY],
        scratch=[pltpu.SemaphoreType.DMA((2,))],
    )
    red1 = jnp.stack([z00, z01, z10, z11]).reshape(2, 2, R1, K)

    colour = ((lax.axis_index("bx") % 2) * 2 + lax.axis_index("by") % 2).astype(jnp.int32).reshape(1)
    last = [(3, (0, -1)), (3, (-1, -1))]
    last_jobs = jobs_of(last)

    def solve_parent(interp, piv, skel, red):
        diff = red - dot(interp[0, 0], skel.astype(BF16))
        return dot(piv[0, 0], diff.astype(BF16)).astype(BF16)

    def join_body(me, pick, interp, piv, couple, za, zb, arrived, children, skel_out, red_out, z_out):
        zs = [za, zb]
        parts = []
        for n in range(4):
            acc = children[n]
            if n < 2:
                acc = acc - arrived[n * S1 : (n + 1) * S1].astype(F32)
            for k, at in last_jobs[n]:
                acc = acc - dot_t(couple[BOXES[n][0], BOXES[n][1], k], zs[at][...])
            parts.append(acc)
        x = jnp.concatenate(parts, axis=0)
        high = x.astype(BF16)
        low = (x - high.astype(F32)).astype(BF16)
        parent = dot(pick[...], high) + dot(pick[...], low)
        skel_out[...] = parent[:S2]
        red_out[...] = parent[S2:]

        @pl.when(me[0] == 0)
        def _():
            z_out[...] = solve_parent(interp, piv, parent[:S2], parent[S2:])

    skel, red, z0 = call(
        join_body,
        [colour, pick, interp2, pivinv2, couple1, *[have[key] for key in last], from_above, skels],
        [PAR_S, PAR_R, PAR_Z],
        specs=[SMEM],
    )

    def sides(z, colours):
        return shift(z, (0, 1), colours), shift(z, (0, -1), colours)

    def ends(up, down, colours):
        return shift(up, (-1, 0), colours), shift(down, (1, 0), colours)

    def parent_body(c, ks, n_sums, me, interp, piv, couple, skel, red, *rest):
        zs, sums = rest[: len(ks)], rest[len(ks) : len(ks) + n_sums]
        *held, z_out, skel_out = rest[len(ks) + n_sums :]
        if held:

            @pl.when(me[0] == c - 1)
            def _():
                z_out[...] = held[0][...]

        @pl.when(me[0] != c)
        def _():
            skel_out[...] = skel[...]

        @pl.when(me[0] == c)
        def _():
            acc = skel[...]
            for x in sums:
                acc = acc - x[...].astype(F32)
            for k, z in zip(ks, zs):
                acc = acc - dot(couple[0, 0, k], z[...])
            skel_out[...] = acc
            z_out[...] = solve_parent(interp, piv, acc, red[...])

    def parent(c, skel, ks, zs, sums=(), held=()):
        return call(
            functools.partial(parent_body, c, ks, len(sums)),
            [colour, interp2, pivinv2, couple2, skel, red, *zs, *sums, *held],
            [PAR_Z, PAR_S],
            specs=[SMEM],
        )

    def row_body(colours, me, above, below, *rest):
        values, (up_out, down_out) = rest[:-2], rest[-2:]
        for n, c in enumerate(colours):

            @pl.when(me[0] == c)
            def _():
                a, own, b = (v[...] for v in values[3 * n : 3 * n + 3])
                for w, out in ((above, up_out), (below, down_out)):
                    out[...] = (dot(w[0], a) + dot(w[1], own) + dot(w[2], b)).astype(BF16)

    def row(colours, values):
        return call(
            functools.partial(row_body, colours),
            [colour, above_mats, below_mats, *values],
            [PAR_M, PAR_M],
            specs=[SMEM],
        )

    side0 = sides(z0, (0,))
    z1, skel = parent(1, skel, [3, 4], side0)
    corners = [shift(z1, (-OFFSETS[k][0], -OFFSETS[k][1]), (1,)) for k in CORNERS]
    (below_pack, above_pack), z0 = after([below_pack, above_pack], z0)
    above_mats = shift(below_pack, (1, 0), (0, 1, 3))
    below_mats = shift(above_pack, (-1, 0), (0, 1, 3))
    from_below, from_above = ends(z0, z0, (0,))
    z2, skel = parent(2, skel, [*ENDS, *CORNERS], [from_above, from_below, *corners], held=[z1])
    side2 = sides(z2, (1, 2))
    sums1 = ends(*row((1,), (side0[0], z1, side0[1])), (1,))
    z3, skel = parent(3, skel, [3, 4], side2, sums1)
    side3 = sides(z3, (3,))
    values = (side3[0], z2, side3[1], side2[0], z3, side2[1])
    end1 = ends(*row((2, 3), values), (2, 3))

    def early_body(me, interp, couple, skel, z0, z1, z2, z3, al, ar, bl, br, skel_out, z_out):
        for c, own in enumerate((z0, z1, z2, z3)):

            @pl.when(me[0] == c)
            def _():
                zc = own[...]
                z_out[...] = zc
                acc = skel[...] - dot_t(interp[0, 0], zc)
                if c % 2 == 0:
                    xl, xr = ((al, ar), (bl, br))[c // 2]
                    acc = acc - (dot(couple[0, 0, 3], xl[...]) + dot(couple[0, 0, 4], xr[...]))
                skel_out[...] = acc

    skel, red2 = call(
        early_body, [colour, interp2, couple2, skel, z0, z1, z2, z3, *side2, *side3], [PAR_S, PAR_Z], specs=[SMEM]
    )

    def late_body(me, skel, a, b, skel_out):
        @pl.when(me[0] < 2)
        def _():
            skel_out[...] = skel[...] - (a[...].astype(F32) + b[...].astype(F32))

        @pl.when(me[0] >= 2)
        def _():
            skel_out[...] = skel[...]

    (skel2,) = call(late_body, [colour, skel, *end1], [PAR_S], specs=[SMEM])
    return (red1, red2[None, None], skel2[None, None])


def solution(mesh):
    in_specs = (
        P("bx", "by", None, None),
        P("bx", "by", None),
        P("bx", "by", None, None),
        P("bx", "by", None, None),
        P("bx", "by", None, None, None),
        P("bx", "by", None),
        P("bx", "by", None, None),
        P("bx", "by", None, None),
        P("bx", "by", None, None, None),
    )
    out_specs = (P("bx", "by", None, None), P("bx", "by", None, None), P("bx", "by", None, None))
    return jax.shard_map(work, mesh=mesh, in_specs=in_specs, out_specs=out_specs, check_vma=False)
```
